32 devices in a mesh: grp: 2 (over y), seq: 4 (over z), section: 2 (over x), head: 2 (over core).
Axes of the slice: x: 2, y: 2, z: 4, core: 2. Of those that a mesh axis runs over, the one named last changes fastest.
Arguments:
- queries: bfloat16 [2048, 2048], P(('grp', 'seq'), ('section', 'head')), parts along dimension 0, may hold values from -6 to 6
- reflect_keys: bfloat16 [2048, 2, 2048], P(('grp', 'seq'), None, ('section', 'head')), parts along dimension 0, may hold values from -6 to 6
- reflect_values: bfloat16 [2048, 2, 2048], P(('grp', 'seq'), None, ('section', 'head')), parts along dimension 0, may hold values from -6 to 6
- reflect_betas: float32 [2048, 2, 16], P(('grp', 'seq'), None, ('section', 'head')), parts along dimension 0, may hold values from 0 to 2
- decay_rates: float32 [2048, 16], P(('grp', 'seq'), ('section', 'head')), parts along dimension 0, may hold values from 0 to 1
- resets: int32 [2048], P(('grp', 'seq')), parts along dimension 0, may hold values 0 or 1
- out_weight: bfloat16 [2048, 2048], P(('section', 'head')), may hold values from -0.125 to 0.125
- out_cotangent: bfloat16 [2048, 2048], P(('grp', 'seq'), ('section', 'head')), parts along dimension 0, may hold values from -6 to 6
Outputs:
- output_features: bfloat16 [2048, 2048], P(('section', 'head'), ('grp', 'seq')), parts along dimension 1
- value_grads: float32 [2048, 2, 2048], P(('grp', 'seq'), None, ('section', 'head')), parts along dimension 0
The draws below stay inside these ranges and needn't reach their ends.
There are 2 independent parts, one for each index of `grp`. The reference program is written for one: setup_inputs(seed, part) draws one part's arguments, and reference() takes and returns one part's arrays. A program takes and returns all parts, laid end to end along the dimension named above; an argument that names none is the same for every part. Nothing has to cross between parts.
Inputs may be any that keep to these rules, and one draw needn't show every extreme that they name: `resets`: 1 marks a token before which the state is cleared.
All inputs are finite; a program needn't handle non-finite values. No bound on the sum of `resets` on one device may be relied on, other than what follows from the above.
Results may differ from the reference program's by a relative error of at most 0.005.
Values may be sent and summed in bfloat16 or wider, within the bound.
A program may use at most 128 MiB of HBM per device.

```python
import math
import jax
import jax.numpy as jnp
from jax import lax

D = 2048
HEAD_COUNT = 16
HEAD_DIM = 128
TOK_DEV = 256
TOKEN_LENGTH = 1024


def head_slow(source, slow_count):
    head_order = jax.random.permutation(jax.random.fold_in(source, 101), HEAD_COUNT)
    return (head_order < slow_count).astype(jnp.float32)


def log_uniform(source, dims_shape, low_end, high_end):
    return jnp.exp(jax.random.uniform(source, dims_shape, jnp.float32, math.log(low_end), math.log(high_end)))


def draw_decay_rates(key, part):
    slow_count = HEAD_COUNT // 2
    slow_low = 0.1
    slow_high = 0.4
    slow_mask = head_slow(key, slow_count)
    slow_level = log_uniform(jax.random.fold_in(key, 1), (HEAD_COUNT,), slow_low, slow_high) / TOKEN_LENGTH
    fast_level = log_uniform(jax.random.fold_in(key, 2), (HEAD_COUNT,), 0.02, 0.05)
    baseline_intensity = slow_mask * slow_level + (1.0 - slow_mask) * fast_level
    token_multiplier = log_uniform(jax.random.fold_in(key, 3), (TOKEN_LENGTH, HEAD_COUNT), 0.5, 2.0)
    block_draw = log_uniform(jax.random.fold_in(key, 4), (TOKEN_LENGTH // TOK_DEV, HEAD_COUNT), 0.5, 2.0)
    block_multiplier = jnp.repeat(block_draw, TOK_DEV, axis=0)
    first_spike = jax.random.randint(jax.random.fold_in(key, 5), (HEAD_COUNT,), 0, TOKEN_LENGTH)
    spike_offset = jax.random.randint(jax.random.fold_in(key, 9), (HEAD_COUNT,), 1, TOKEN_LENGTH)
    second_spike = (first_spike + spike_offset) % TOKEN_LENGTH
    spike_position = jnp.stack([first_spike, second_spike], axis=0)
    spike_retention = jax.random.uniform(jax.random.fold_in(key, 6), (2, HEAD_COUNT), jnp.float32, 0.5, 0.8)
    token_positions = jnp.arange(TOKEN_LENGTH)[:, None, None]
    spike_intensity = jnp.sum(jnp.where(token_positions == spike_position[None], -jnp.log(spike_retention)[None], 0.0), axis=1)
    return (baseline_intensity[None, :] * token_multiplier * block_multiplier + spike_intensity).astype(jnp.float32)


def draw_reflect_betas(key, part):
    slow_count = HEAD_COUNT // 2
    fast_low = 0.3
    fast_high = 1.5
    slow_low = 0.4
    slow_high = 1.6
    slow_mask = head_slow(key, slow_count)
    slow_beta = 0.3 * HEAD_DIM / TOKEN_LENGTH * jax.random.uniform(jax.random.fold_in(key, 7), (TOKEN_LENGTH, 2, HEAD_COUNT), jnp.float32, slow_low, slow_high)
    fast_beta = jax.random.uniform(jax.random.fold_in(key, 8), (TOKEN_LENGTH, 2, HEAD_COUNT), jnp.float32, fast_low, fast_high)
    return jnp.where(slow_mask[None, None, :] > 0.5, slow_beta, fast_beta).astype(jnp.float32)


def touch_ends(entries, key, low, high):
    longest = entries.shape.index(max(entries.shape))
    spots = []
    for shift in (0, 1):
        where = [jax.random.randint(jax.random.fold_in(key, axis), (), 0, length) for axis, length in enumerate(entries.shape)]
        where[longest] = (where[longest] + shift) % entries.shape[longest]
        spots.append(tuple(where))
    return entries.at[spots[0]].set(low).at[spots[1]].set(high)


def steps_of(key, shape, cuts, smallest, high):
    level = 1.0
    for axis_at, blocks in cuts:
        heights = jax.random.uniform(jax.random.fold_in(jax.random.fold_in(key, 6), axis_at), (blocks,), jnp.float32, smallest / len(cuts), high / len(cuts))
        level = level * jnp.repeat(jnp.exp(heights), shape[axis_at] // blocks).reshape((-1,) + (1,) * (len(shape) - 1 - axis_at))
    return level


def bell_draw(key, dims, deviation, most, pieces=(), dtype=jnp.bfloat16):
    drawn = deviation * jax.random.normal(key, dims, jnp.float32)
    if pieces:
        drawn = drawn * steps_of(key, dims, pieces, -0.22, 0.18)
    return jnp.clip(drawn, -most, most).astype(dtype)


def setup_inputs(seed: int = 0, part: int = 0) -> dict:
    keys = jax.random.split(jax.random.key(seed), 9)
    part_splits = jax.random.split(jax.random.fold_in(keys[8], part), 9)
    queries = bell_draw(part_splits[0], (TOKEN_LENGTH, HEAD_COUNT * HEAD_DIM), 1.0, 6.0, ((0, 4), (1, 4)))
    reflect_keys = bell_draw(part_splits[1], (TOKEN_LENGTH, 2, HEAD_COUNT * HEAD_DIM), 1.0, 6.0, ((0, 4), (2, 4)))
    reflect_values = bell_draw(part_splits[2], (TOKEN_LENGTH, 2, HEAD_COUNT * HEAD_DIM), 1.0, 6.0, ((0, 4), (2, 4)))
    reflect_betas = draw_reflect_betas(jax.random.fold_in(jax.random.fold_in(keys[8], part), 71), part)
    decay_rates = draw_decay_rates(jax.random.fold_in(jax.random.fold_in(keys[8], part), 71), part)
    resets = touch_ends((jax.random.randint(part_splits[5], (TOKEN_LENGTH,), 0, TOKEN_LENGTH) < 2).astype(jnp.int32), jax.random.fold_in(part_splits[5], 1), 0, 1)
    out_weight = bell_draw(keys[6], (HEAD_COUNT * HEAD_DIM, D), (HEAD_COUNT * HEAD_DIM) ** -0.5, 0.125, ((0, 4),))
    out_cotangent = bell_draw(part_splits[7], (TOKEN_LENGTH, D), 1.0, 6.0, ((0, 4), (1, 4)))
    return {"queries": queries, "reflect_keys": reflect_keys, "reflect_values": reflect_values, "reflect_betas": reflect_betas, "decay_rates": decay_rates, "resets": resets, "out_weight": out_weight, "out_cotangent": out_cotangent}


MATMUL_ACCURACY = lax.Precision.HIGHEST

def normalize(raw):
    floats = raw.astype(jnp.float32)
    return floats * lax.rsqrt(lax.optimization_barrier(jnp.sum(floats * floats, axis=-1, keepdims=True)) + 1e-06)

def reflect(state_matrix, factor, beta, reflect_direction):
    projected_state = jnp.einsum('to,tof->tf', reflect_direction, state_matrix, precision=MATMUL_ACCURACY)
    return factor[:, None, None] * (state_matrix - beta[:, None, None] * reflect_direction[:, :, None] * projected_state[:, None, :])

def reference(queries, reflect_keys, reflect_values, reflect_betas, decay_rates, resets, out_weight, out_cotangent):
    queries_f = queries.astype(jnp.float32).reshape(TOKEN_LENGTH, HEAD_COUNT, HEAD_DIM)
    unit_keys = normalize(reflect_keys.reshape(TOKEN_LENGTH, 2, HEAD_COUNT, HEAD_DIM))
    values_f = reflect_values.astype(jnp.float32).reshape(TOKEN_LENGTH, 2, HEAD_COUNT, HEAD_DIM)
    gates = jnp.exp(-decay_rates)
    survive = jnp.broadcast_to((1 - resets).astype(jnp.float32)[:, None], (TOKEN_LENGTH, HEAD_COUNT))
    zeros_state = jnp.zeros((HEAD_COUNT, HEAD_DIM, HEAD_DIM), jnp.float32)

    def forward_token(state_matrix, inputs):
        query_vector, paired_keys, values_pair, paired_betas, gate, alive = inputs
        for member, factor in ((0, alive), (1, gate)):
            written = (paired_betas[member][:, None] * paired_keys[member])[:, :, None] * values_pair[member][:, None, :]
            state_matrix = reflect(state_matrix, factor, paired_betas[member], paired_keys[member]) + written
        return (state_matrix, jnp.einsum('to,tof->tf', query_vector, state_matrix, precision=MATMUL_ACCURACY))
    _, mixed_heads = lax.scan(forward_token, zeros_state, (queries_f, unit_keys, values_f, reflect_betas, gates, survive))
    heads_bf = mixed_heads.reshape(TOKEN_LENGTH, HEAD_COUNT * HEAD_DIM).astype(jnp.bfloat16)
    output_features = jnp.dot(heads_bf, out_weight, preferred_element_type=jnp.float32).astype(jnp.bfloat16).T
    upstream = jnp.dot(out_cotangent, out_weight.T, preferred_element_type=jnp.float32).reshape(TOKEN_LENGTH, HEAD_COUNT, HEAD_DIM)

    def backward_token(carried, inputs):
        query_vector, paired_keys, paired_betas, gate, alive, incoming = inputs
        second_reflection = carried + query_vector[:, :, None] * incoming[:, None, :]
        gradient_second = paired_betas[1][:, None] * jnp.einsum('to,tof->tf', paired_keys[1], second_reflection, precision=MATMUL_ACCURACY)
        first_reflection = reflect(second_reflection, gate, paired_betas[1], paired_keys[1])
        gradient_first = paired_betas[0][:, None] * jnp.einsum('to,tof->tf', paired_keys[0], first_reflection, precision=MATMUL_ACCURACY)
        carried = reflect(first_reflection, alive, paired_betas[0], paired_keys[0])
        return (carried, jnp.stack([gradient_first, gradient_second], axis=0))
    _, gradient = lax.scan(backward_token, zeros_state, (queries_f, unit_keys, reflect_betas, gates, survive, upstream), reverse=True)
    value_grads = gradient.reshape(TOKEN_LENGTH, 2, HEAD_COUNT * HEAD_DIM)
    return (output_features, value_grads)
```

```python
import functools
import jax
import jax.numpy as jnp
from jax import lax
from jax.experimental import pallas as pl
from jax.experimental.pallas import tpu as pltpu
from jax.sharding import PartitionSpec as P

HALF = 64
BLK = 2 * HALF
F32 = jnp.float32
BF16 = jnp.bfloat16
NN = (((1,), (0,)), ((), ()))
NT = (((1,), (1,)), ((), ()))
TN = (((0,), (0,)), ((), ()))


def dot1(a, b, dims=NN):
    return lax.dot_general(a.astype(BF16), b.astype(BF16), dims, preferred_element_type=F32)


def halves(a):
    high = a.astype(BF16)
    return high, (a - high.astype(F32)).astype(BF16)


def dot3(a, b, dims=NN):
    ah, al = halves(a)
    bh, bl = halves(b)
    d = functools.partial(lax.dot_general, dimension_numbers=dims, preferred_element_type=F32)
    return d(ah, bh) + (d(ah, bl) + d(al, bh))


def iota(shape, axis):
    return lax.broadcasted_iota(jnp.int32, shape, axis)


def step_token(index):
    block, rest = index // BLK, index % BLK
    return block * HALF + rest % HALF, rest // HALF


def local_kernel(rows_ref, cols_ref, q_ref, k0_ref, k1_ref, v0_ref, v1_ref,
                 y_ref, r_ref, m_ref, o_ref, b_ref):
    tokens, width = q_ref.shape
    blocks = tokens // HALF
    steps = 2 * tokens
    rows, cols = rows_ref[0], cols_ref[0]
    tok_s, ref_s = step_token(iota((tokens, steps), 1))
    source = iota((tokens, steps), 0)
    upto = (source <= tok_s).astype(F32)
    before = jnp.where(ref_s == 1, upto, (source < tok_s).astype(F32))
    high = functools.partial(lax.dot_general, precision=lax.Precision.HIGHEST,
                             preferred_element_type=F32)
    c_row = high(rows[:, :tokens], before, NN)[0:1]
    z_row = high(rows[:, :tokens], upto, NN)[1:2]
    beta_row = rows[2:3, tokens:]
    tok_c, ref_c = step_token(iota((steps, tokens), 0))
    source_c = iota((steps, tokens), 1)
    upto_c = (source_c <= tok_c).astype(F32)
    before_c = jnp.where(ref_c == 1, upto_c, (source_c < tok_c).astype(F32))
    c_col = high(before_c, cols[:tokens], NN)[:, 0:1]
    z_col = high(upto_c, cols[:tokens], NN)[:, 1:2]
    beta_col = cols[tokens:, 2:3]
    c_end, z_end = c_row[:, steps - 1:], z_row[:, steps - 1:]
    gamma_row = jnp.where(z_row == 0, jnp.exp(-c_row), 0.0)
    gamma_end_row = jnp.where(z_row == z_end, jnp.exp(c_row - c_end), 0.0)
    gamma_end = jnp.where(z_end == 0, jnp.exp(-c_end), 0.0)

    def sl(b):
        return slice(b * BLK, (b + 1) * BLK)

    keys, values = [], []
    for b in range(blocks):
        t = slice(b * HALF, (b + 1) * HALF)
        keys.append(jnp.concatenate([k0_ref[t, :], k1_ref[t, :]], axis=0))
        values.append(jnp.concatenate([v0_ref[t, :], v1_ref[t, :]], axis=0))
    eye = iota((BLK, BLK), 0) == iota((BLK, BLK), 1)
    tm_r = 2 * (iota((BLK, BLK), 0) % HALF) + iota((BLK, BLK), 0) // HALF
    tm_c = 2 * (iota((BLK, BLK), 1) % HALF) + iota((BLK, BLK), 1) // HALF

    gram = [[dot1(keys[b], keys[c], NT) for c in range(b + 1)] for b in range(blocks)]
    scale_row, scale_col = [], []
    for b in range(blocks):
        diag = jnp.where(eye, gram[b][b], 0.0)
        scale_row.append(lax.rsqrt(jnp.sum(diag, axis=0, keepdims=True) + 1e-6))
        scale_col.append(lax.rsqrt(jnp.sum(diag, axis=1, keepdims=True) + 1e-6))

    low = [[None] * blocks for _ in range(blocks)]
    for b in range(blocks):
        left = beta_col[sl(b)] * scale_col[b]
        for c in range(b + 1):
            valid = z_col[sl(b)] == z_row[:, sl(c)]
            if b == c:
                valid = valid & (tm_r > tm_c)
            gap = jnp.where(valid, c_row[:, sl(c)] - c_col[sl(b)], 0.0)
            low[b][c] = jnp.where(valid, jnp.exp(gap) * gram[b][c] * left * scale_row[c], 0.0)

    inverse = [jnp.where(eye, 1.0, 0.0) - jnp.where((tm_r >> 1) == (tm_c >> 1), low[b][b], 0.0)
               for b in range(blocks)]
    level = 2
    while (1 << level) <= BLK:
        pick = ((tm_r >> level) == (tm_c >> level)) & ((tm_r >> (level - 1)) != (tm_c >> (level - 1)))
        inner = [dot3(jnp.where(pick, low[b][b], 0.0), inverse[b]) for b in range(blocks)]
        inverse = [inverse[b] - dot3(inverse[b], inner[b]) for b in range(blocks)]
        level += 1

    solved = [None] * blocks
    for b in reversed(range(blocks)):
        parts = []
        kq_scale = scale_row[b]
        for a in range(b, blocks):
            t = slice(a * HALF, (a + 1) * HALF)
            product = dot1(q_ref[t, :], keys[b], NT)
            second = slice(a * BLK + HALF, (a + 1) * BLK)
            valid = z_col[second] == z_row[:, sl(b)]
            if a == b:
                valid = valid & (iota((HALF, BLK), 0) >= iota((HALF, BLK), 1) % HALF)
            gap = jnp.where(valid, c_row[:, sl(b)] - c_col[second], 0.0)
            parts.append(jnp.where(valid, jnp.exp(gap) * product * kq_scale, 0.0))
        parts.append(keys[b].astype(F32).T * (kq_scale * gamma_end_row[:, sl(b)]))
        x = jnp.concatenate(parts, axis=0)
        if b + 1 < blocks:
            later = []
            for c in range(b + 1, blocks):
                y = solved[c]
                later.append(jnp.concatenate([jnp.zeros(((c - b) * HALF, BLK), F32), y], axis=0))
            x = x - dot3(jnp.concatenate(later, axis=1),
                         jnp.concatenate([low[c][b] for c in range(b + 1, blocks)], axis=0))
        solved[b] = dot3(x, inverse[b])

    total = tokens + width
    plain = jnp.zeros((total, width), F32)
    moved = jnp.zeros((total, width), F32)
    for b in range(blocks):
        y = solved[b] * beta_row[:, sl(b)]
        if b:
            y = jnp.concatenate([jnp.zeros((b * HALF, BLK), F32), y], axis=0)
        y_ref[0, :, sl(b)] = y.astype(BF16)
        plain = plain + dot1(y, values[b])
        moved = moved + dot1(y * (gamma_row[:, sl(b)] * scale_row[b]), keys[b])
    o_ref[0] = plain[:tokens]
    b_ref[0] = plain[tokens:]
    gamma_tok = []
    for a in range(blocks):
        second = slice(a * BLK + HALF, (a + 1) * BLK)
        gamma_tok.append(jnp.where(z_col[second] == 0, jnp.exp(-c_col[second]), 0.0))
    gamma_tok = jnp.concatenate(gamma_tok, axis=0)
    r_ref[0] = (gamma_tok * q_ref[...].astype(F32) - moved[:tokens]).astype(BF16)
    m_ref[0] = jnp.where(iota((width, width), 0) == iota((width, width), 1), gamma_end, 0.0) - moved[tokens:]


def adjoint_kernel(cot_ref, w_ref, r_ref, up_ref, d_ref):
    up = dot1(cot_ref[...], w_ref[...], NT).astype(BF16)
    up_ref[0] = up
    d_ref[0] = dot1(r_ref[0], up, TN)


def finish_kernel(r_ref, o_ref, s_ref, y_ref, up_ref, ds_ref, mixed_ref, g0_ref, g1_ref):
    tokens, width = mixed_ref.shape
    mixed_ref[...] = (dot1(r_ref[0], s_ref[0]) + o_ref[0]).astype(BF16)
    right = jnp.concatenate([up_ref[0], ds_ref[0].astype(BF16)], axis=0)
    grad = dot1(y_ref[0], right, TN)
    for b in range(tokens // HALF):
        t = slice(b * HALF, (b + 1) * HALF)
        g0_ref[t, :] = grad[b * BLK:b * BLK + HALF]
        g1_ref[t, :] = grad[b * BLK + HALF:(b + 1) * BLK]


def step_order(array):
    tokens, _, heads = array.shape
    return array.reshape(tokens // HALF, HALF, 2, heads).transpose(3, 0, 2, 1).reshape(heads, 2 * tokens)


def per_device(queries, reflect_keys, reflect_values, reflect_betas, decay_rates, resets,
               out_weight, out_cotangent):
    tokens = queries.shape[0]
    heads = reflect_betas.shape[2]
    width = queries.shape[1] // heads
    steps = 2 * tokens
    devices = lax.axis_size("seq")

    cot = lax.all_gather(out_cotangent, ("section", "head"), axis=1, tiled=True)

    resets_f = jnp.broadcast_to(resets.astype(F32)[None, :], (heads, tokens))
    front = jnp.stack([decay_rates.T, resets_f, jnp.zeros_like(resets_f)], axis=1)
    betas = step_order(reflect_betas)
    back = jnp.stack([jnp.zeros_like(betas), jnp.zeros_like(betas), betas], axis=1)
    rows = jnp.concatenate([front, back], axis=2)
    rows = jnp.pad(rows, ((0, 0), (0, 5), (0, 0)))
    cols = rows.transpose(0, 2, 1)
    keys2 = reflect_keys.reshape(tokens, 2 * heads * width)
    values2 = reflect_values.reshape(tokens, 2 * heads * width)

    def whole(*shape):
        return pl.BlockSpec((1,) + shape, lambda h: (h,) + (0,) * len(shape))

    def column(offset):
        return pl.BlockSpec((tokens, width), lambda h: (0, h + offset))

    total = tokens + width
    y, r, m, o, b = pl.pallas_call(
        local_kernel,
        grid=(heads,),
        in_specs=[whole(8, tokens + steps), whole(tokens + steps, 8), column(0),
                  column(0), column(heads), column(0), column(heads)],
        out_specs=[whole(total, steps), whole(tokens, width), whole(width, width),
                   whole(tokens, width), whole(width, width)],
        out_shape=[jax.ShapeDtypeStruct((heads, total, steps), BF16),
                   jax.ShapeDtypeStruct((heads, tokens, width), BF16),
                   jax.ShapeDtypeStruct((heads, width, width), F32),
                   jax.ShapeDtypeStruct((heads, tokens, width), F32),
                   jax.ShapeDtypeStruct((heads, width, width), F32)],
        compiler_params=pltpu.CompilerParams(vmem_limit_bytes=48 << 20),
        cost_estimate=pl.CostEstimate(flops=8 << 30, bytes_accessed=8 << 20, transcendentals=0),
        name="local",
    )(rows, cols, queries, keys2, keys2, values2, values2)

    up, d = pl.pallas_call(
        adjoint_kernel,
        grid=(heads,),
        in_specs=[pl.BlockSpec(cot.shape, lambda h: (0, 0)),
                  pl.BlockSpec((width, out_weight.shape[1]), lambda h: (h, 0)),
                  whole(tokens, width)],
        out_specs=[whole(tokens, width), whole(width, width)],
        out_shape=[jax.ShapeDtypeStruct((heads, tokens, width), BF16),
                   jax.ShapeDtypeStruct((heads, width, width), F32)],
        compiler_params=pltpu.CompilerParams(vmem_limit_bytes=32 << 20),
        name="adjoint",
    )(cot, out_weight, r)

    batched = functools.partial(lax.dot_general, precision=lax.Precision.HIGH,
                                preferred_element_type=F32)
    state = jnp.zeros((heads, width, width), BF16)
    adjoint = jnp.zeros((heads, width, width), BF16)
    for hop in range(devices - 1):
        out = batched(m, state.astype(F32), (((2,), (1,)), ((0,), (0,)))) + b
        back_out = batched(m, adjoint.astype(F32), (((1,), (1,)), ((0,), (0,)))) + d
        state = state + lax.ppermute(out.astype(BF16), "seq", [(hop, hop + 1)])
        adjoint = adjoint + lax.ppermute(
            back_out.astype(BF16), "seq", [(devices - 1 - hop, devices - 2 - hop)])

    flat = jax.ShapeDtypeStruct((tokens, heads * width), F32)
    mixed, g0, g1 = pl.pallas_call(
        finish_kernel,
        grid=(heads,),
        in_specs=[whole(tokens, width), whole(tokens, width), whole(width, width),
                  whole(total, steps), whole(tokens, width), whole(width, width)],
        out_specs=[column(0), column(0), column(0)],
        out_shape=[jax.ShapeDtypeStruct((tokens, heads * width), BF16), flat, flat],
        compiler_params=pltpu.CompilerParams(vmem_limit_bytes=32 << 20),
        name="finish",
    )(r, o, state, y, up, adjoint)
    value_grads = jnp.stack([g0, g1], axis=1)

    partial = lax.dot_general(out_weight, mixed, (((0,), (1,)), ((), ())), preferred_element_type=F32)
    output = lax.psum_scatter(partial, ("section", "head"), scatter_dimension=0, tiled=True)
    return output.astype(BF16), value_grads


def solution(mesh):
    return jax.shard_map(
        per_device,
        mesh=mesh,
        in_specs=(
            P(("grp", "seq"), ("section", "head")),
            P(("grp", "seq"), None, ("section", "head")),
            P(("grp", "seq"), None, ("section", "head")),
            P(("grp", "seq"), None, ("section", "head")),
            P(("grp", "seq"), ("section", "head")),
            P(("grp", "seq")),
            P(("section", "head"), None),
            P(("grp", "seq"), ("section", "head")),
        ),
        out_specs=(
            P(("section", "head"), ("grp", "seq")),
            P(("grp", "seq"), None, ("section", "head")),
        ),
        check_vma=False,
    )
```

```python
import functools
import jax
import jax.numpy as jnp
from jax import lax
from jax.experimental import pallas as pl
from jax.experimental.pallas import tpu as pltpu
from jax.sharding import PartitionSpec as P

HALF = 64
BLK = 2 * HALF
F32 = jnp.float32
BF16 = jnp.bfloat16
NN = (((1,), (0,)), ((), ()))
NT = (((1,), (1,)), ((), ()))
TN = (((0,), (0,)), ((), ()))


def dot1(a, b, dims=NN):
    return lax.dot_general(a.astype(BF16), b.astype(BF16), dims, preferred_element_type=F32)


def halves(a):
    high = a.astype(BF16)
    return high, (a - high.astype(F32)).astype(BF16)


def dot3(a, b, dims=NN):
    ah, al = halves(a)
    bh, bl = halves(b)
    d = functools.partial(lax.dot_general, dimension_numbers=dims, preferred_element_type=F32)
    return d(ah, bh) + (d(ah, bl) + d(al, bh))


def iota(shape, axis):
    return lax.broadcasted_iota(jnp.int32, shape, axis)


def step_token(index):
    block, rest = index // BLK, index % BLK
    return block * HALF + rest % HALF, rest // HALF


def local_kernel(rows_ref, cols_ref, q_ref, k0_ref, k1_ref, v0_ref, v1_ref,
                 y_ref, r_ref, m_ref, o_ref, b_ref):
    tokens, width = q_ref.shape
    blocks = tokens // HALF
    steps = 2 * tokens
    rows, cols = rows_ref[0], cols_ref[0]
    tok_s, ref_s = step_token(iota((tokens, steps), 1))
    source = iota((tokens, steps), 0)
    upto = (source <= tok_s).astype(F32)
    before = jnp.where(ref_s == 1, upto, (source < tok_s).astype(F32))
    high = functools.partial(lax.dot_general, precision=lax.Precision.HIGHEST,
                             preferred_element_type=F32)
    c_row = high(rows[:, :tokens], before, NN)[0:1]
    z_row = high(rows[:, :tokens], upto, NN)[1:2]
    beta_row = rows[2:3, tokens:]
    tok_c, ref_c = step_token(iota((steps, tokens), 0))
    source_c = iota((steps, tokens), 1)
    upto_c = (source_c <= tok_c).astype(F32)
    before_c = jnp.where(ref_c == 1, upto_c, (source_c < tok_c).astype(F32))
    c_col = high(before_c, cols[:tokens], NN)[:, 0:1]
    z_col = high(upto_c, cols[:tokens], NN)[:, 1:2]
    beta_col = cols[tokens:, 2:3]
    c_end, z_end = c_row[:, steps - 1:], z_row[:, steps - 1:]
    gamma_row = jnp.where(z_row == 0, jnp.exp(-c_row), 0.0)
    gamma_end_row = jnp.where(z_row == z_end, jnp.exp(c_row - c_end), 0.0)
    gamma_end = jnp.where(z_end == 0, jnp.exp(-c_end), 0.0)

    def sl(b):
        return slice(b * BLK, (b + 1) * BLK)

    keys, values = [], []
    for b in range(blocks):
        t = slice(b * HALF, (b + 1) * HALF)
        keys.append(jnp.concatenate([k0_ref[t, :], k1_ref[t, :]], axis=0))
        values.append(jnp.concatenate([v0_ref[t, :], v1_ref[t, :]], axis=0))
    eye = iota((BLK, BLK), 0) == iota((BLK, BLK), 1)
    tm_r = 2 * (iota((BLK, BLK), 0) % HALF) + iota((BLK, BLK), 0) // HALF
    tm_c = 2 * (iota((BLK, BLK), 1) % HALF) + iota((BLK, BLK), 1) // HALF

    gram = [[dot1(keys[b], keys[c], NT) for c in range(b + 1)] for b in range(blocks)]
    scale_row, scale_col = [], []
    for b in range(blocks):
        diag = jnp.where(eye, gram[b][b], 0.0)
        scale_row.append(lax.rsqrt(jnp.sum(diag, axis=0, keepdims=True) + 1e-6))
        scale_col.append(lax.rsqrt(jnp.sum(diag, axis=1, keepdims=True) + 1e-6))

    low = [[None] * blocks for _ in range(blocks)]
    for b in range(blocks):
        left = beta_col[sl(b)] * scale_col[b]
        for c in range(b + 1):
            valid = z_col[sl(b)] == z_row[:, sl(c)]
            if b == c:
                valid = valid & (tm_r > tm_c)
            gap = jnp.where(valid, c_row[:, sl(c)] - c_col[sl(b)], 0.0)
            low[b][c] = jnp.where(valid, jnp.exp(gap) * gram[b][c] * left * scale_row[c], 0.0)

    inverse = [jnp.where(eye, 1.0, 0.0) - jnp.where((tm_r >> 1) == (tm_c >> 1), low[b][b], 0.0)
               for b in range(blocks)]
    level = 2
    while (1 << level) <= BLK:
        pick = ((tm_r >> level) == (tm_c >> level)) & ((tm_r >> (level - 1)) != (tm_c >> (level - 1)))
        inner = [dot3(jnp.where(pick, low[b][b], 0.0), inverse[b]) for b in range(blocks)]
        inverse = [inverse[b] - dot3(inverse[b], inner[b]) for b in range(blocks)]
        level += 1

    solved = [None] * blocks
    for b in reversed(range(blocks)):
        parts = []
        kq_scale = scale_row[b]
        for a in range(b, blocks):
            t = slice(a * HALF, (a + 1) * HALF)
            product = dot1(q_ref[t, :], keys[b], NT)
            second = slice(a * BLK + HALF, (a + 1) * BLK)
            valid = z_col[second] == z_row[:, sl(b)]
            if a == b:
                valid = valid & (iota((HALF, BLK), 0) >= iota((HALF, BLK), 1) % HALF)
            gap = jnp.where(valid, c_row[:, sl(b)] - c_col[second], 0.0)
            parts.append(jnp.where(valid, jnp.exp(gap) * product * kq_scale, 0.0))
        parts.append(keys[b].astype(F32).T * (kq_scale * gamma_end_row[:, sl(b)]))
        x = jnp.concatenate(parts, axis=0)
        if b + 1 < blocks:
            later = []
            for c in range(b + 1, blocks):
                y = solved[c]
                later.append(jnp.concatenate([jnp.zeros(((c - b) * HALF, BLK), F32), y], axis=0))
            x = x - dot3(jnp.concatenate(later, axis=1),
                         jnp.concatenate([low[c][b] for c in range(b + 1, blocks)], axis=0))
        solved[b] = dot3(x, inverse[b])

    total = tokens + width
    plain = jnp.zeros((total, width), F32)
    moved = jnp.zeros((total, width), F32)
    for b in range(blocks):
        y = solved[b] * beta_row[:, sl(b)]
        if b:
            y = jnp.concatenate([jnp.zeros((b * HALF, BLK), F32), y], axis=0)
        y_ref[0, :, sl(b)] = y.astype(BF16)
        plain = plain + dot1(y, values[b])
        moved = moved + dot1(y * (gamma_row[:, sl(b)] * scale_row[b]), keys[b])
    o_ref[0] = plain[:tokens]
    b_ref[0] = plain[tokens:]
    gamma_tok = []
    for a in range(blocks):
        second = slice(a * BLK + HALF, (a + 1) * BLK)
        gamma_tok.append(jnp.where(z_col[second] == 0, jnp.exp(-c_col[second]), 0.0))
    gamma_tok = jnp.concatenate(gamma_tok, axis=0)
    r_ref[0] = (gamma_tok * q_ref[...].astype(F32) - moved[:tokens]).astype(BF16)
    m_ref[0] = jnp.where(iota((width, width), 0) == iota((width, width), 1), gamma_end, 0.0) - moved[tokens:]


def adjoint_kernel(cot_ref, w_ref, r_ref, up_ref, d_ref):
    up = dot1(cot_ref[...], w_ref[...], NT).astype(BF16)
    up_ref[0] = up
    d_ref[0] = dot1(r_ref[0], up, TN)


MESH = pl.DeviceIdType.MESH


def chain_kernel(devices, m_ref, b_ref, d_ref, s_ref, ds_ref, s_in, s_out, ds_in, ds_out,
                 s_sent, s_got, ds_sent, ds_got):
    heads = m_ref.shape[0]
    place = lax.axis_index("seq")
    first, last = place == 0, place == devices - 1
    barrier = pltpu.get_barrier_semaphore()

    @pl.when(jnp.logical_not(first))
    def _():
        pl.semaphore_signal(barrier, inc=1, device_id={"seq": place - 1}, device_id_type=MESH)

    @pl.when(jnp.logical_not(last))
    def _():
        pl.semaphore_signal(barrier, inc=1, device_id={"seq": place + 1}, device_id_type=MESH)

    if devices > 1:
        pl.semaphore_wait(barrier, jnp.where(first | last, 1, 2))

    def up(h):
        return pltpu.make_async_remote_copy(
            src_ref=s_out.at[h], dst_ref=s_in.at[h], send_sem=s_sent.at[h], recv_sem=s_got.at[h],
            device_id={"seq": place + 1}, device_id_type=MESH)

    def down(h):
        return pltpu.make_async_remote_copy(
            src_ref=ds_out.at[h], dst_ref=ds_in.at[h], send_sem=ds_sent.at[h], recv_sem=ds_got.at[h],
            device_id={"seq": place - 1}, device_id_type=MESH)

    def forward():
        for h in range(heads):
            @pl.when(first)
            def _():
                s_in[h] = jnp.zeros(s_in.shape[1:], BF16)

            @pl.when(jnp.logical_not(first))
            def _():
                up(h).wait_recv()

            @pl.when(jnp.logical_not(last))
            def _():
                mh, ml = halves(m_ref[h])
                s = s_in[h]
                s_out[h] = (dot1(mh, s) + dot1(ml, s) + b_ref[h]).astype(BF16)
                up(h).start()

            s_ref[h] = s_in[h]

    def backward():
        for h in range(heads):
            @pl.when(last)
            def _():
                ds_in[h] = jnp.zeros(ds_in.shape[1:], BF16)

            @pl.when(jnp.logical_not(last))
            def _():
                down(h).wait_recv()

            @pl.when(jnp.logical_not(first))
            def _():
                mh, ml = halves(m_ref[h])
                ds = ds_in[h]
                ds_out[h] = (dot1(mh, ds, TN) + dot1(ml, ds, TN) + d_ref[h]).astype(BF16)
                down(h).start()

            ds_ref[h] = ds_in[h]

    low = 2 * place < devices

    @pl.when(low)
    def _():
        forward()
        backward()

    @pl.when(jnp.logical_not(low))
    def _():
        backward()
        forward()

    @pl.when(jnp.logical_not(last))
    def _():
        for h in range(heads):
            up(h).wait_send()

    @pl.when(jnp.logical_not(first))
    def _():
        for h in range(heads):
            down(h).wait_send()


def output_kernel(sections, r_ref, o_ref, s_ref, y_ref, up_ref, ds_ref, w_ref,
                  out_ref, g0_ref, g1_ref,
                  mixed, pair_out, pair_in, cross_out, cross_in,
                  pair_sent, pair_got, cross_sent, cross_got):
    heads, tokens, width = r_ref.shape
    features = out_ref.shape[0]
    section, core = lax.axis_index("section"), lax.axis_index("head")
    sibling = 1 - core

    def peer(k):
        return lax.rem(section + k, sections)

    barrier = pltpu.get_barrier_semaphore()
    pl.semaphore_signal(barrier, inc=1, device_id={"head": sibling}, device_id_type=MESH)
    for k in range(1, sections):
        pl.semaphore_signal(barrier, inc=1, device_id={"section": peer(k)}, device_id_type=MESH)

    for h in range(heads):
        mixed[h * width:(h + 1) * width, :] = (dot1(r_ref[h], s_ref[h]) + o_ref[h]).T.astype(BF16)
    pl.semaphore_wait(barrier, sections)

    def partial(target, side):
        start = pl.multiple_of((target * 2 + side) * features, 128)
        return dot1(w_ref[:, pl.ds(start, features)], mixed[...], TN)

    def pair(k):
        return pltpu.make_async_remote_copy(
            src_ref=pair_out.at[k], dst_ref=pair_in.at[k], send_sem=pair_sent.at[k],
            recv_sem=pair_got.at[k], device_id={"head": sibling}, device_id_type=MESH)

    def cross(k):
        return pltpu.make_async_remote_copy(
            src_ref=cross_out.at[k - 1], dst_ref=cross_in.at[k - 1], send_sem=cross_sent.at[k - 1],
            recv_sem=cross_got.at[k - 1], device_id={"section": peer(k)}, device_id_type=MESH)

    order = list(range(1, sections)) + [0]
    for k in order:
        pair_out[k] = partial(peer(k), sibling)
        pair(k).start()
    for k in range(1, sections):
        mine = partial(peer(k), core)
        pair(k).wait_recv()
        cross_out[k - 1] = (mine + pair_in[k]).astype(BF16)
        cross(k).start()
    for h in range(heads):
        right = jnp.concatenate([up_ref[h], ds_ref[h]], axis=0)
        grad = dot1(y_ref[h], right, TN)
        lanes = slice(h * width, (h + 1) * width)
        for b in range(tokens // HALF):
            t = slice(b * HALF, (b + 1) * HALF)
            g0_ref[t, lanes] = grad[b * BLK:b * BLK + HALF]
            g1_ref[t, lanes] = grad[b * BLK + HALF:(b + 1) * BLK]
    total = partial(section, core)
    pair(0).wait_recv()
    total = total + pair_in[0]
    for k in range(1, sections):
        cross(k).wait_recv()
        total = total + cross_in[k - 1].astype(F32)
    out_ref[...] = total.astype(BF16)
    for k in order:
        pair(k).wait_send()
    for k in range(1, sections):
        cross(k).wait_send()


def step_order(array):
    tokens, _, heads = array.shape
    return array.reshape(tokens // HALF, HALF, 2, heads).transpose(3, 0, 2, 1).reshape(heads, 2 * tokens)


def per_device(queries, reflect_keys, reflect_values, reflect_betas, decay_rates, resets,
               out_weight, out_cotangent):
    tokens = queries.shape[0]
    heads = reflect_betas.shape[2]
    width = queries.shape[1] // heads
    steps = 2 * tokens
    devices = lax.axis_size("seq")

    cot = lax.all_gather(out_cotangent, ("section", "head"), axis=1, tiled=True)

    resets_f = jnp.broadcast_to(resets.astype(F32)[None, :], (heads, tokens))
    front = jnp.stack([decay_rates.T, resets_f, jnp.zeros_like(resets_f)], axis=1)
    betas = step_order(reflect_betas)
    back = jnp.stack([jnp.zeros_like(betas), jnp.zeros_like(betas), betas], axis=1)
    rows = jnp.concatenate([front, back], axis=2)
    rows = jnp.pad(rows, ((0, 0), (0, 5), (0, 0)))
    cols = rows.transpose(0, 2, 1)
    keys2 = reflect_keys.reshape(tokens, 2 * heads * width)
    values2 = reflect_values.reshape(tokens, 2 * heads * width)

    def whole(*shape):
        return pl.BlockSpec((1,) + shape, lambda h: (h,) + (0,) * len(shape))

    def column(offset):
        return pl.BlockSpec((tokens, width), lambda h: (0, h + offset))

    total = tokens + width
    y, r, m, o, b = pl.pallas_call(
        local_kernel,
        grid=(heads,),
        in_specs=[whole(8, tokens + steps), whole(tokens + steps, 8), column(0),
                  column(0), column(heads), column(0), column(heads)],
        out_specs=[whole(total, steps), whole(tokens, width), whole(width, width),
                   whole(tokens, width), whole(width, width)],
        out_shape=[jax.ShapeDtypeStruct((heads, total, steps), BF16),
                   jax.ShapeDtypeStruct((heads, tokens, width), BF16),
                   jax.ShapeDtypeStruct((heads, width, width), F32),
                   jax.ShapeDtypeStruct((heads, tokens, width), F32),
                   jax.ShapeDtypeStruct((heads, width, width), F32)],
        compiler_params=pltpu.CompilerParams(vmem_limit_bytes=48 << 20),
        cost_estimate=pl.CostEstimate(flops=8 << 30, bytes_accessed=8 << 20, transcendentals=0),
        name="local",
    )(rows, cols, queries, keys2, keys2, values2, values2)

    up, d = pl.pallas_call(
        adjoint_kernel,
        grid=(heads,),
        in_specs=[pl.BlockSpec(cot.shape, lambda h: (0, 0)),
                  pl.BlockSpec((width, out_weight.shape[1]), lambda h: (h, 0)),
                  whole(tokens, width)],
        out_specs=[whole(tokens, width), whole(width, width)],
        out_shape=[jax.ShapeDtypeStruct((heads, tokens, width), BF16),
                   jax.ShapeDtypeStruct((heads, width, width), F32)],
        compiler_params=pltpu.CompilerParams(vmem_limit_bytes=32 << 20),
        name="adjoint",
    )(cot, out_weight, r)

    square = (heads, width, width)
    vmem = pl.BlockSpec(memory_space=pltpu.VMEM)
    dma = pltpu.SemaphoreType.DMA
    state, adjoint = pl.pallas_call(
        functools.partial(chain_kernel, devices),
        in_specs=[vmem] * 3,
        out_specs=[vmem] * 2,
        out_shape=[jax.ShapeDtypeStruct(square, BF16)] * 2,
        scratch_shapes=[pltpu.VMEM(square, BF16)] * 4 + [dma((heads,))] * 4,
        compiler_params=pltpu.CompilerParams(
            collective_id=0, has_side_effects=True, vmem_limit_bytes=32 << 20),
        name="chain",
    )(m, b, d)

    sections = lax.axis_size("section")
    features = out_weight.shape[1] // (2 * sections)
    flat = jax.ShapeDtypeStruct((tokens, heads * width), F32)
    output, g0, g1 = pl.pallas_call(
        functools.partial(output_kernel, sections),
        in_specs=[vmem] * 7,
        out_specs=[vmem] * 3,
        out_shape=[jax.ShapeDtypeStruct((features, tokens), BF16), flat, flat],
        scratch_shapes=[pltpu.VMEM((heads * width, tokens), BF16),
                        pltpu.VMEM((sections, features, tokens), F32),
                        pltpu.VMEM((sections, features, tokens), F32),
                        pltpu.VMEM((sections - 1, features, tokens), BF16),
                        pltpu.VMEM((sections - 1, features, tokens), BF16),
                        dma((sections,)), dma((sections,)), dma((sections - 1,)), dma((sections - 1,))],
        compiler_params=pltpu.CompilerParams(
            collective_id=1, has_side_effects=True, vmem_limit_bytes=48 << 20),
        name="output",
    )(r, o, state, y, up, adjoint, out_weight)
    return output, jnp.stack([g0, g1], axis=1)


def solution(mesh):
    return jax.shard_map(
        per_device,
        mesh=mesh,
        in_specs=(
            P(("grp", "seq"), ("section", "head")),
            P(("grp", "seq"), None, ("section", "head")),
            P(("grp", "seq"), None, ("section", "head")),
            P(("grp", "seq"), None, ("section", "head")),
            P(("grp", "seq"), ("section", "head")),
            P(("grp", "seq")),
            P(("section", "head"), None),
            P(("grp", "seq"), ("section", "head")),
        ),
        out_specs=(
            P(("section", "head"), ("grp", "seq")),
            P(("grp", "seq"), None, ("section", "head")),
        ),
        check_vma=False,
    )
```

```python
import functools
import jax
import jax.numpy as jnp
from jax import lax
from jax.experimental import pallas as pl
from jax.experimental.pallas import tpu as pltpu
from jax.sharding import PartitionSpec as P

HALF = 64
BLK = 2 * HALF
F32 = jnp.float32
BF16 = jnp.bfloat16
NN = (((1,), (0,)), ((), ()))
NT = (((1,), (1,)), ((), ()))
TN = (((0,), (0,)), ((), ()))


def dot1(a, b, dims=NN):
    return lax.dot_general(a.astype(BF16), b.astype(BF16), dims, preferred_element_type=F32)


def halves(a):
    high = a.astype(BF16)
    return high, (a - high.astype(F32)).astype(BF16)


def dot3(a, b, dims=NN):
    ah, al = halves(a)
    bh, bl = halves(b)
    d = functools.partial(lax.dot_general, dimension_numbers=dims, preferred_element_type=F32)
    return d(ah, bh) + (d(ah, bl) + d(al, bh))


def iota(shape, axis):
    return lax.broadcasted_iota(jnp.int32, shape, axis)


def step_token(index):
    block, rest = index // BLK, index % BLK
    return block * HALF + rest % HALF, rest // HALF


def local_kernel(rows_ref, q_ref, k0_ref, k1_ref, v0_ref, v1_ref,
                 y_ref, r_ref, m_ref, o_ref, b_ref):
    group, width = m_ref.shape[0], m_ref.shape[1]
    tokens = q_ref.shape[0]
    blocks = tokens // HALF
    steps = 2 * tokens
    everything = [(g, b) for g in range(group) for b in range(blocks)]
    rows = rows_ref[0]
    top = rows.astype(BF16)
    rest = rows - top.astype(F32)
    middle = rest.astype(BF16)
    bottom = (rest - middle.astype(F32)).astype(BF16)
    tok_s, ref_s = step_token(iota((tokens, steps), 1))
    source = iota((tokens, steps), 0)
    upto = (source <= tok_s).astype(F32)
    before = (source <= tok_s + ref_s - 1).astype(F32)
    sums = dot1(jnp.concatenate([top.astype(F32), middle.astype(F32), bottom.astype(F32)], axis=0), before)
    c_rows = sums[0:8] + sums[8:16] + sums[16:24]
    z_rows = dot1(rows, upto)
    beta_rows = []
    for g in range(group):
        first, second = rows[1 + group + g:2 + group + g], rows[1 + 2 * group + g:2 + 2 * group + g]
        pieces = []
        for b in range(blocks):
            t = slice(b * HALF, (b + 1) * HALF)
            pieces += [first[:, t], second[:, t]]
        beta_rows.append(jnp.concatenate(pieces, axis=1))
    z_row = z_rows[group:group + 1]
    packed = jnp.concatenate(
        [c_rows[0:group], z_row] + beta_rows + [jnp.zeros((7 - 2 * group, steps), F32)], axis=0)
    packed_cols = packed.T
    z_col = packed_cols[:, group:group + 1]
    c_row = [c_rows[g:g + 1] for g in range(group)]
    c_col = [packed_cols[:, g:g + 1] for g in range(group)]
    beta_col = [packed_cols[:, group + 1 + g:group + 2 + g] for g in range(group)]
    z_end = z_row[:, steps - 1:]

    def sl(b):
        return slice(b * BLK, (b + 1) * BLK)

    def lanes(g):
        return slice(g * width, (g + 1) * width)

    keys, values = {}, {}
    for g, b in everything:
        t = slice(b * HALF, (b + 1) * HALF)
        keys[g, b] = jnp.concatenate([k0_ref[t, lanes(g)], k1_ref[t, lanes(g)]], axis=0)
        values[g, b] = jnp.concatenate([v0_ref[t, lanes(g)], v1_ref[t, lanes(g)]], axis=0)
    eye = iota((BLK, BLK), 0) == iota((BLK, BLK), 1)
    identity = jnp.where(eye, 1.0, 0.0)
    tm_r = 2 * (iota((BLK, BLK), 0) % HALF) + iota((BLK, BLK), 0) // HALF
    tm_c = 2 * (iota((BLK, BLK), 1) % HALF) + iota((BLK, BLK), 1) // HALF

    low, scale_row, scale_col, gram = {}, {}, {}, {}
    for g, b in everything:
        for c in range(b + 1):
            gram[g, b, c] = dot1(keys[g, b], keys[g, c], NT)
    for g, b in everything:
        diag = jnp.where(eye, gram[g, b, b], 0.0)
        scale_row[g, b] = lax.rsqrt(jnp.sum(diag, axis=0, keepdims=True) + 1e-6)
        scale_col[g, b] = lax.rsqrt(jnp.sum(diag, axis=1, keepdims=True) + 1e-6)
    for g, b in everything:
        left = beta_col[g][sl(b)] * scale_col[g, b]
        for c in range(b + 1):
            valid = z_col[sl(b)] == z_row[:, sl(c)]
            if b == c:
                valid = valid & (tm_r > tm_c)
            gap = jnp.where(valid, c_row[g][:, sl(c)] - c_col[g][sl(b)], 0.0)
            low[g, b, c] = jnp.where(
                valid, jnp.exp(gap) * gram[g, b, c] * left * scale_row[g, c], 0.0)

    rounded = {i: low[i[0], i[1], i[1]].astype(BF16) for i in everything}
    inverse = {i: identity - jnp.where((tm_r >> 1) == (tm_c >> 1), low[i[0], i[1], i[1]], 0.0)
               for i in everything}
    level = 2
    while (1 << level) <= BLK:
        pick = ((tm_r >> level) == (tm_c >> level)) & ((tm_r >> (level - 1)) != (tm_c >> (level - 1)))
        narrow = {i: inverse[i].astype(BF16) for i in everything}
        inner = {i: dot1(jnp.where(pick, rounded[i], jnp.zeros_like(rounded[i])), narrow[i])
                 for i in everything}
        inverse = {i: inverse[i] - dot1(narrow[i], inner[i]) for i in everything}
        level += 1
    for _ in range(2):
        residual = {i: dot3(low[i[0], i[1], i[1]], inverse[i]) + (inverse[i] - identity)
                    for i in everything}
        inverse = {i: inverse[i] - dot1(inverse[i], residual[i]) for i in everything}

    gamma_end_row = [jnp.where(z_row == z_end, jnp.exp(c_row[g] - c_row[g][:, steps - 1:]), 0.0)
                     for g in range(group)]
    solved = {}
    for b in reversed(range(blocks)):
        for g in range(group):
            parts = []
            for a in range(b, blocks):
                t = slice(a * HALF, (a + 1) * HALF)
                product = dot1(q_ref[t, lanes(g)], keys[g, b], NT)
                second = slice(a * BLK + HALF, (a + 1) * BLK)
                valid = z_col[second] == z_row[:, sl(b)]
                if a == b:
                    valid = valid & (iota((HALF, BLK), 0) >= iota((HALF, BLK), 1) % HALF)
                gap = jnp.where(valid, c_row[g][:, sl(b)] - c_col[g][second], 0.0)
                parts.append(jnp.where(valid, jnp.exp(gap) * product * scale_row[g, b], 0.0))
            parts.append(keys[g, b].astype(F32).T * (scale_row[g, b] * gamma_end_row[g][:, sl(b)]))
            x = jnp.concatenate(parts, axis=0)
            if b + 1 < blocks:
                later = []
                for c in range(b + 1, blocks):
                    later.append(jnp.concatenate(
                        [jnp.zeros(((c - b) * HALF, BLK), F32), solved[g, c]], axis=0))
                x = x - dot3(jnp.concatenate(later, axis=1),
                             jnp.concatenate([low[g, c, b] for c in range(b + 1, blocks)], axis=0))
            solved[g, b] = dot3(x, inverse[g, b])

    total = tokens + width
    for g in range(group):
        gamma_row = jnp.where(z_row == 0, jnp.exp(-c_row[g]), 0.0)
        plain, moved, gamma_tok = [], [], []
        for b in range(blocks):
            y = solved[g, b] * packed[group + 1 + g:group + 2 + g, sl(b)]
            if b:
                y = jnp.concatenate([jnp.zeros((b * HALF, BLK), F32), y], axis=0)
            y_ref[g, :, sl(b)] = y.astype(BF16)
            plain.append(y.astype(BF16))
            moved.append((y * (gamma_row[:, sl(b)] * scale_row[g, b])).astype(BF16))
            second = slice(b * BLK + HALF, (b + 1) * BLK)
            gamma_tok.append(jnp.where(z_col[second] == 0, jnp.exp(-c_col[g][second]), 0.0))
        plain = dot1(jnp.concatenate(plain, axis=1),
                     jnp.concatenate([values[g, b] for b in range(blocks)], axis=0))
        moved = dot1(jnp.concatenate(moved, axis=1),
                     jnp.concatenate([keys[g, b] for b in range(blocks)], axis=0))
        o_ref[g] = plain[:tokens]
        b_ref[g] = plain[tokens:]
        gamma_tok = jnp.concatenate(gamma_tok, axis=0)
        r_ref[g] = (gamma_tok * q_ref[:, lanes(g)].astype(F32) - moved[:tokens]).astype(BF16)
        gamma_end = jnp.where(z_end == 0, jnp.exp(-c_row[g][:, steps - 1:]), 0.0)
        m_ref[g] = jnp.where(iota((width, width), 0) == iota((width, width), 1), gamma_end, 0.0) - moved[tokens:]


def adjoint_kernel(cot_ref, w_ref, r_ref, up_ref, d_ref):
    up = dot1(cot_ref[...], w_ref[...], NT).astype(BF16)
    up_ref[0] = up
    d_ref[0] = dot1(r_ref[0], up, TN)


MESH = pl.DeviceIdType.MESH


def chain_kernel(devices, m_ref, b_ref, d_ref, s_ref, ds_ref, s_in, s_out, ds_in, ds_out,
                 s_sent, s_got, ds_sent, ds_got):
    heads = m_ref.shape[0]
    place = lax.axis_index("seq")
    first, last = place == 0, place == devices - 1
    barrier = pltpu.get_barrier_semaphore()

    @pl.when(jnp.logical_not(first))
    def _():
        pl.semaphore_signal(barrier, inc=1, device_id={"seq": place - 1}, device_id_type=MESH)

    @pl.when(jnp.logical_not(last))
    def _():
        pl.semaphore_signal(barrier, inc=1, device_id={"seq": place + 1}, device_id_type=MESH)

    if devices > 1:
        pl.semaphore_wait(barrier, jnp.where(first | last, 1, 2))

    def up(h):
        return pltpu.make_async_remote_copy(
            src_ref=s_out.at[h], dst_ref=s_in.at[h], send_sem=s_sent.at[h], recv_sem=s_got.at[h],
            device_id={"seq": place + 1}, device_id_type=MESH)

    def down(h):
        return pltpu.make_async_remote_copy(
            src_ref=ds_out.at[h], dst_ref=ds_in.at[h], send_sem=ds_sent.at[h], recv_sem=ds_got.at[h],
            device_id={"seq": place - 1}, device_id_type=MESH)

    def forward():
        for h in range(heads):
            @pl.when(first)
            def _():
                s_in[h] = jnp.zeros(s_in.shape[1:], BF16)

            @pl.when(jnp.logical_not(first))
            def _():
                up(h).wait_recv()

            @pl.when(jnp.logical_not(last))
            def _():
                mh, ml = halves(m_ref[h])
                s = s_in[h]
                s_out[h] = (dot1(mh, s) + dot1(ml, s) + b_ref[h]).astype(BF16)
                up(h).start()

            s_ref[h] = s_in[h]

    def backward():
        for h in range(heads):
            @pl.when(last)
            def _():
                ds_in[h] = jnp.zeros(ds_in.shape[1:], BF16)

            @pl.when(jnp.logical_not(last))
            def _():
                down(h).wait_recv()

            @pl.when(jnp.logical_not(first))
            def _():
                mh, ml = halves(m_ref[h])
                ds = ds_in[h]
                ds_out[h] = (dot1(mh, ds, TN) + dot1(ml, ds, TN) + d_ref[h]).astype(BF16)
                down(h).start()

            ds_ref[h] = ds_in[h]

    low = 2 * place < devices

    @pl.when(low)
    def _():
        forward()
        backward()

    @pl.when(jnp.logical_not(low))
    def _():
        backward()
        forward()

    @pl.when(jnp.logical_not(last))
    def _():
        for h in range(heads):
            up(h).wait_send()

    @pl.when(jnp.logical_not(first))
    def _():
        for h in range(heads):
            down(h).wait_send()


def output_kernel(sections, r_ref, o_ref, s_ref, y_ref, up_ref, ds_ref, w_ref,
                  out_ref, g_ref,
                  mixed, pair_out, pair_in, cross_out, cross_in,
                  pair_sent, pair_got, cross_sent, cross_got):
    heads, tokens, width = r_ref.shape
    features = out_ref.shape[0]
    section, core = lax.axis_index("section"), lax.axis_index("head")
    sibling = 1 - core

    def peer(k):
        return lax.rem(section + k, sections)

    barrier = pltpu.get_barrier_semaphore()
    pl.semaphore_signal(barrier, inc=1, device_id={"head": sibling}, device_id_type=MESH)
    for k in range(1, sections):
        pl.semaphore_signal(barrier, inc=1, device_id={"section": peer(k)}, device_id_type=MESH)

    for h in range(heads):
        mixed[h * width:(h + 1) * width, :] = (dot1(r_ref[h], s_ref[h]) + o_ref[h]).T.astype(BF16)
    pl.semaphore_wait(barrier, sections)

    def partial(target, side):
        start = pl.multiple_of((target * 2 + side) * features, 128)
        return dot1(w_ref[:, pl.ds(start, features)], mixed[...], TN)

    def pair(k):
        return pltpu.make_async_remote_copy(
            src_ref=pair_out.at[k], dst_ref=pair_in.at[k], send_sem=pair_sent.at[k],
            recv_sem=pair_got.at[k], device_id={"head": sibling}, device_id_type=MESH)

    def cross(k):
        return pltpu.make_async_remote_copy(
            src_ref=cross_out.at[k - 1], dst_ref=cross_in.at[k - 1], send_sem=cross_sent.at[k - 1],
            recv_sem=cross_got.at[k - 1], device_id={"section": peer(k)}, device_id_type=MESH)

    order = list(range(1, sections)) + [0]
    for k in order:
        pair_out[k] = partial(peer(k), sibling)
        pair(k).start()
    for k in range(1, sections):
        mine = partial(peer(k), core)
        pair(k).wait_recv()
        cross_out[k - 1] = (mine + pair_in[k]).astype(BF16)
        cross(k).start()
    for h in range(heads):
        right = jnp.concatenate([up_ref[h], ds_ref[h]], axis=0)
        grad = dot1(y_ref[h], right, TN)
        lanes = slice(h * width, (h + 1) * width)
        for b in range(tokens // HALF):
            t = slice(b * HALF, (b + 1) * HALF)
            g_ref[t, 0, lanes] = grad[b * BLK:b * BLK + HALF]
            g_ref[t, 1, lanes] = grad[b * BLK + HALF:(b + 1) * BLK]
    total = partial(section, core)
    pair(0).wait_recv()
    total = total + pair_in[0]
    for k in range(1, sections):
        cross(k).wait_recv()
        total = total + cross_in[k - 1].astype(F32)
    out_ref[...] = total.astype(BF16)
    for k in order:
        pair(k).wait_send()
    for k in range(1, sections):
        cross(k).wait_send()


def per_device(queries, reflect_keys, reflect_values, reflect_betas, decay_rates, resets,
               out_weight, out_cotangent):
    tokens = queries.shape[0]
    heads = reflect_betas.shape[2]
    width = queries.shape[1] // heads
    steps = 2 * tokens
    devices = lax.axis_size("seq")

    cot = lax.all_gather(out_cotangent, ("section", "head"), axis=1, tiled=True)

    group = 2 if heads % 2 == 0 else 1
    groups = heads // group
    marks = jnp.broadcast_to(resets.astype(F32)[None, None, :], (groups, 1, tokens))
    betas = reflect_betas.transpose(1, 2, 0).reshape(2, groups, group, tokens)
    rows = jnp.concatenate(
        [decay_rates.T.reshape(groups, group, tokens), marks, betas[0], betas[1],
         jnp.zeros((groups, 7 - 3 * group, tokens), F32)], axis=1)
    keys2 = reflect_keys.reshape(tokens, 2 * heads * width)
    values2 = reflect_values.reshape(tokens, 2 * heads * width)

    def whole(*shape):
        return pl.BlockSpec((1,) + shape, lambda h: (h,) + (0,) * len(shape))

    def several(*shape):
        return pl.BlockSpec((group,) + shape, lambda h: (h,) + (0,) * len(shape))

    def columns(offset):
        return pl.BlockSpec((tokens, group * width), lambda h: (0, h + offset))

    total = tokens + width
    y, r, m, o, b = pl.pallas_call(
        local_kernel,
        grid=(groups,),
        in_specs=[whole(8, tokens), columns(0), columns(0), columns(groups), columns(0), columns(groups)],
        out_specs=[several(total, steps), several(tokens, width), several(width, width),
                   several(tokens, width), several(width, width)],
        out_shape=[jax.ShapeDtypeStruct((heads, total, steps), BF16),
                   jax.ShapeDtypeStruct((heads, tokens, width), BF16),
                   jax.ShapeDtypeStruct((heads, width, width), F32),
                   jax.ShapeDtypeStruct((heads, tokens, width), F32),
                   jax.ShapeDtypeStruct((heads, width, width), F32)],
        compiler_params=pltpu.CompilerParams(vmem_limit_bytes=48 << 20),
        cost_estimate=pl.CostEstimate(flops=8 << 30, bytes_accessed=8 << 20, transcendentals=0),
        name="local",
    )(rows, queries, keys2, keys2, values2, values2)

    up, d = pl.pallas_call(
        adjoint_kernel,
        grid=(heads,),
        in_specs=[pl.BlockSpec(cot.shape, lambda h: (0, 0)),
                  pl.BlockSpec((width, out_weight.shape[1]), lambda h: (h, 0)),
                  whole(tokens, width)],
        out_specs=[whole(tokens, width), whole(width, width)],
        out_shape=[jax.ShapeDtypeStruct((heads, tokens, width), BF16),
                   jax.ShapeDtypeStruct((heads, width, width), F32)],
        compiler_params=pltpu.CompilerParams(vmem_limit_bytes=32 << 20),
        name="adjoint",
    )(cot, out_weight, r)

    square = (heads, width, width)
    vmem = pl.BlockSpec(memory_space=pltpu.VMEM)
    dma = pltpu.SemaphoreType.DMA
    state, adjoint = pl.pallas_call(
        functools.partial(chain_kernel, devices),
        in_specs=[vmem] * 3,
        out_specs=[vmem] * 2,
        out_shape=[jax.ShapeDtypeStruct(square, BF16)] * 2,
        scratch_shapes=[pltpu.VMEM(square, BF16)] * 4 + [dma((heads,))] * 4,
        compiler_params=pltpu.CompilerParams(
            collective_id=0, has_side_effects=True, vmem_limit_bytes=32 << 20),
        name="chain",
    )(m, b, d)

    sections = lax.axis_size("section")
    features = out_weight.shape[1] // (2 * sections)
    output, value_grads = pl.pallas_call(
        functools.partial(output_kernel, sections),
        in_specs=[vmem] * 7,
        out_specs=[vmem] * 2,
        out_shape=[jax.ShapeDtypeStruct((features, tokens), BF16),
                   jax.ShapeDtypeStruct((tokens, 2, heads * width), F32)],
        scratch_shapes=[pltpu.VMEM((heads * width, tokens), BF16),
                        pltpu.VMEM((sections, features, tokens), F32),
                        pltpu.VMEM((sections, features, tokens), F32),
                        pltpu.VMEM((sections - 1, features, tokens), BF16),
                        pltpu.VMEM((sections - 1, features, tokens), BF16),
                        dma((sections,)), dma((sections,)), dma((sections - 1,)), dma((sections - 1,))],
        compiler_params=pltpu.CompilerParams(
            collective_id=1, has_side_effects=True, vmem_limit_bytes=48 << 20),
        name="output",
    )(r, o, state, y, up, adjoint, out_weight)
    return output, value_grads


def solution(mesh):
    return jax.shard_map(
        per_device,
        mesh=mesh,
        in_specs=(
            P(("grp", "seq"), ("section", "head")),
            P(("grp", "seq"), None, ("section", "head")),
            P(("grp", "seq"), None, ("section", "head")),
            P(("grp", "seq"), None, ("section", "head")),
            P(("grp", "seq"), ("section", "head")),
            P(("grp", "seq")),
            P(("section", "head"), None),
            P(("grp", "seq"), ("section", "head")),
        ),
        out_specs=(
            P(("section", "head"), ("grp", "seq")),
            P(("grp", "seq"), None, ("section", "head")),
        ),
        check_vma=False,
    )
```

```python
import functools
import jax
import jax.numpy as jnp
from jax import lax
from jax.experimental import pallas as pl
from jax.experimental.pallas import tpu as pltpu
from jax.sharding import PartitionSpec as P

HALF = 64
BLK = 2 * HALF
F32 = jnp.float32
BF16 = jnp.bfloat16
NN = (((1,), (0,)), ((), ()))
NT = (((1,), (1,)), ((), ()))
TN = (((0,), (0,)), ((), ()))


def dot1(a, b, dims=NN):
    return lax.dot_general(a.astype(BF16), b.astype(BF16), dims, preferred_element_type=F32)


def halves(a):
    high = a.astype(BF16)
    return high, (a - high.astype(F32)).astype(BF16)


def dot3(a, b, dims=NN):
    ah, al = halves(a)
    bh, bl = halves(b)
    d = functools.partial(lax.dot_general, dimension_numbers=dims, preferred_element_type=F32)
    return d(ah, bh) + (d(ah, bl) + d(al, bh))


def iota(shape, axis):
    return lax.broadcasted_iota(jnp.int32, shape, axis)


def step_token(index):
    block, rest = index // BLK, index % BLK
    return block * HALF + rest % HALF, rest // HALF


def local_kernel(rows_ref, q_ref, k0_ref, k1_ref, v0_ref, v1_ref,
                 y_ref, r_ref, m_ref, o_ref, b_ref):
    group, width = m_ref.shape[0], m_ref.shape[1]
    tokens = q_ref.shape[0]
    blocks = tokens // HALF
    steps = 2 * tokens
    everything = [(g, b) for g in range(group) for b in range(blocks)]
    rows = rows_ref[0]
    top = rows.astype(BF16)
    rest = rows - top.astype(F32)
    middle = rest.astype(BF16)
    bottom = (rest - middle.astype(F32)).astype(BF16)
    tok_s, ref_s = step_token(iota((tokens, steps), 1))
    source = iota((tokens, steps), 0)
    upto = (source <= tok_s).astype(F32)
    before = (source <= tok_s + ref_s - 1).astype(F32)
    sums = dot1(jnp.concatenate([top.astype(F32), middle.astype(F32), bottom.astype(F32)], axis=0), before)
    c_rows = sums[0:8] + sums[8:16] + sums[16:24]
    z_rows = dot1(rows, upto)
    beta_rows = []
    for g in range(group):
        first, second = rows[1 + group + g:2 + group + g], rows[1 + 2 * group + g:2 + 2 * group + g]
        pieces = []
        for b in range(blocks):
            t = slice(b * HALF, (b + 1) * HALF)
            pieces += [first[:, t], second[:, t]]
        beta_rows.append(jnp.concatenate(pieces, axis=1))
    z_row = z_rows[group:group + 1]
    packed = jnp.concatenate(
        [c_rows[0:group], z_row] + beta_rows + [jnp.zeros((7 - 2 * group, steps), F32)], axis=0)
    packed_cols = packed.T
    z_col = packed_cols[:, group:group + 1]
    c_row = [c_rows[g:g + 1] for g in range(group)]
    c_col = [packed_cols[:, g:g + 1] for g in range(group)]
    beta_col = [packed_cols[:, group + 1 + g:group + 2 + g] for g in range(group)]
    z_end = z_row[:, steps - 1:]

    def sl(b):
        return slice(b * BLK, (b + 1) * BLK)

    def lanes(g):
        return slice(g * width, (g + 1) * width)

    keys, values = {}, {}
    for g, b in everything:
        t = slice(b * HALF, (b + 1) * HALF)
        keys[g, b] = jnp.concatenate([k0_ref[t, lanes(g)], k1_ref[t, lanes(g)]], axis=0)
        values[g, b] = jnp.concatenate([v0_ref[t, lanes(g)], v1_ref[t, lanes(g)]], axis=0)
    eye = iota((BLK, BLK), 0) == iota((BLK, BLK), 1)
    identity = jnp.where(eye, 1.0, 0.0)
    tm_r = 2 * (iota((BLK, BLK), 0) % HALF) + iota((BLK, BLK), 0) // HALF
    tm_c = 2 * (iota((BLK, BLK), 1) % HALF) + iota((BLK, BLK), 1) // HALF

    low, scale_row, scale_col, gram = {}, {}, {}, {}
    for g, b in everything:
        for c in range(b + 1):
            gram[g, b, c] = dot1(keys[g, b], keys[g, c], NT)
    for g, b in everything:
        diag = jnp.where(eye, gram[g, b, b], 0.0)
        scale_row[g, b] = lax.rsqrt(jnp.sum(diag, axis=0, keepdims=True) + 1e-6)
        scale_col[g, b] = lax.rsqrt(jnp.sum(diag, axis=1, keepdims=True) + 1e-6)
    for g, b in everything:
        left = beta_col[g][sl(b)] * scale_col[g, b]
        for c in range(b + 1):
            valid = z_col[sl(b)] == z_row[:, sl(c)]
            if b == c:
                valid = valid & (tm_r > tm_c)
            gap = jnp.where(valid, c_row[g][:, sl(c)] - c_col[g][sl(b)], 0.0)
            low[g, b, c] = jnp.where(
                valid, jnp.exp(gap) * gram[g, b, c] * left * scale_row[g, c], 0.0)

    rounded = {i: low[i[0], i[1], i[1]].astype(BF16) for i in everything}
    inverse = {i: identity - jnp.where((tm_r >> 1) == (tm_c >> 1), low[i[0], i[1], i[1]], 0.0)
               for i in everything}
    level = 2
    while (1 << level) <= BLK:
        pick = ((tm_r >> level) == (tm_c >> level)) & ((tm_r >> (level - 1)) != (tm_c >> (level - 1)))
        narrow = {i: inverse[i].astype(BF16) for i in everything}
        inner = {i: dot1(jnp.where(pick, rounded[i], jnp.zeros_like(rounded[i])), narrow[i])
                 for i in everything}
        inverse = {i: inverse[i] - dot1(narrow[i], inner[i]) for i in everything}
        level += 1
    for _ in range(2):
        residual = {i: dot3(low[i[0], i[1], i[1]], inverse[i]) + (inverse[i] - identity)
                    for i in everything}
        inverse = {i: inverse[i] - dot1(inverse[i], residual[i]) for i in everything}

    gamma_end_row = [jnp.where(z_row == z_end, jnp.exp(c_row[g] - c_row[g][:, steps - 1:]), 0.0)
                     for g in range(group)]
    solved = {}
    for b in reversed(range(blocks)):
        for g in range(group):
            parts = []
            for a in range(b, blocks):
                t = slice(a * HALF, (a + 1) * HALF)
                product = dot1(q_ref[t, lanes(g)], keys[g, b], NT)
                second = slice(a * BLK + HALF, (a + 1) * BLK)
                valid = z_col[second] == z_row[:, sl(b)]
                if a == b:
                    valid = valid & (iota((HALF, BLK), 0) >= iota((HALF, BLK), 1) % HALF)
                gap = jnp.where(valid, c_row[g][:, sl(b)] - c_col[g][second], 0.0)
                parts.append(jnp.where(valid, jnp.exp(gap) * product * scale_row[g, b], 0.0))
            parts.append(keys[g, b].astype(F32).T * (scale_row[g, b] * gamma_end_row[g][:, sl(b)]))
            x = jnp.concatenate(parts, axis=0)
            if b + 1 < blocks:
                later = []
                for c in range(b + 1, blocks):
                    later.append(jnp.concatenate(
                        [jnp.zeros(((c - b) * HALF, BLK), F32), solved[g, c]], axis=0))
                x = x - dot3(jnp.concatenate(later, axis=1),
                             jnp.concatenate([low[g, c, b] for c in range(b + 1, blocks)], axis=0))
            solved[g, b] = dot3(x, inverse[g, b])

    total = tokens + width
    for g in range(group):
        gamma_row = jnp.where(z_row == 0, jnp.exp(-c_row[g]), 0.0)
        plain, moved, gamma_tok = [], [], []
        for b in range(blocks):
            y = solved[g, b] * packed[group + 1 + g:group + 2 + g, sl(b)]
            if b:
                y = jnp.concatenate([jnp.zeros((b * HALF, BLK), F32), y], axis=0)
            y_ref[g, :, sl(b)] = y.astype(BF16)
            plain.append(y.astype(BF16))
            moved.append((y * (gamma_row[:, sl(b)] * scale_row[g, b])).astype(BF16))
            second = slice(b * BLK + HALF, (b + 1) * BLK)
            gamma_tok.append(jnp.where(z_col[second] == 0, jnp.exp(-c_col[g][second]), 0.0))
        plain = dot1(jnp.concatenate(plain, axis=1),
                     jnp.concatenate([values[g, b] for b in range(blocks)], axis=0))
        moved = dot1(jnp.concatenate(moved, axis=1),
                     jnp.concatenate([keys[g, b] for b in range(blocks)], axis=0))
        o_ref[g] = plain[:tokens]
        b_ref[g] = plain[tokens:]
        gamma_tok = jnp.concatenate(gamma_tok, axis=0)
        r_ref[g] = (gamma_tok * q_ref[:, lanes(g)].astype(F32) - moved[:tokens]).astype(BF16)
        gamma_end = jnp.where(z_end == 0, jnp.exp(-c_row[g][:, steps - 1:]), 0.0)
        m_ref[g] = jnp.where(iota((width, width), 0) == iota((width, width), 1), gamma_end, 0.0) - moved[tokens:]


MESH = pl.DeviceIdType.MESH


def tail_kernel(devices, sections, m_ref, b_ref, r_ref, o_ref, y_ref, cot_ref, w_ref,
                out_ref, g_ref,
                s_in, s_out, ds_in, ds_out, d, up_, mh, ml,
                mixed, pair_out, pair_in, cross_out, cross_in,
                s_sent, s_got, ds_sent, ds_got, pair_sent, pair_got, cross_sent, cross_got):
    heads, tokens, width = r_ref.shape
    features = out_ref.shape[0]
    place = lax.axis_index("seq")
    section, core = lax.axis_index("section"), lax.axis_index("head")
    sibling = 1 - core
    first, last = place == 0, place == devices - 1

    def peer(k):
        return lax.rem(section + k, sections)

    barrier = pltpu.get_barrier_semaphore()

    @pl.when(jnp.logical_not(first))
    def _():
        pl.semaphore_signal(barrier, inc=1, device_id={"seq": place - 1}, device_id_type=MESH)

    @pl.when(jnp.logical_not(last))
    def _():
        pl.semaphore_signal(barrier, inc=1, device_id={"seq": place + 1}, device_id_type=MESH)

    pl.semaphore_signal(barrier, inc=1, device_id={"head": sibling}, device_id_type=MESH)
    for k in range(1, sections):
        pl.semaphore_signal(barrier, inc=1, device_id={"section": peer(k)}, device_id_type=MESH)
    for h in range(heads):
        mh[h], ml[h] = halves(m_ref[h])
    pl.semaphore_wait(barrier, sections + jnp.where(first, 0, 1) + jnp.where(last, 0, 1))

    def up(h):
        return pltpu.make_async_remote_copy(
            src_ref=s_out.at[h], dst_ref=s_in.at[h], send_sem=s_sent.at[h], recv_sem=s_got.at[h],
            device_id={"seq": place + 1}, device_id_type=MESH)

    def down(h):
        return pltpu.make_async_remote_copy(
            src_ref=ds_out.at[h], dst_ref=ds_in.at[h], send_sem=ds_sent.at[h], recv_sem=ds_got.at[h],
            device_id={"seq": place - 1}, device_id_type=MESH)

    def forward():
        for h in range(heads):
            @pl.when(first)
            def _():
                s_in[h] = jnp.zeros(s_in.shape[1:], BF16)

            @pl.when(jnp.logical_not(first))
            def _():
                up(h).wait_recv()

            @pl.when(jnp.logical_not(last))
            def _():
                s = s_in[h]
                s_out[h] = (dot1(mh[h], s) + dot1(ml[h], s) + b_ref[h]).astype(BF16)
                up(h).start()

    def backward():
        for h in range(heads):
            @pl.when(last)
            def _():
                ds_in[h] = jnp.zeros(ds_in.shape[1:], BF16)

            @pl.when(jnp.logical_not(last))
            def _():
                down(h).wait_recv()

            @pl.when(jnp.logical_not(first))
            def _():
                ds = ds_in[h]
                ds_out[h] = (dot1(mh[h], ds, TN) + dot1(ml[h], ds, TN) + d[h]).astype(BF16)
                down(h).start()

    low = 2 * place < devices

    @pl.when(low)
    def _():
        forward()

    for h in range(heads):
        upstream = dot1(cot_ref[...], w_ref[h * width:(h + 1) * width, :], NT).astype(BF16)
        up_[h] = upstream
        d[h] = dot1(r_ref[h], upstream, TN)

    @pl.when(low)
    def _():
        backward()

    @pl.when(jnp.logical_not(low))
    def _():
        backward()
        forward()

    for h in range(heads):
        mixed[h * width:(h + 1) * width, :] = (dot1(r_ref[h], s_in[h]) + o_ref[h]).T.astype(BF16)

    def partial(target, side):
        start = pl.multiple_of((target * 2 + side) * features, 128)
        return dot1(w_ref[:, pl.ds(start, features)], mixed[...], TN)

    def pair(k):
        return pltpu.make_async_remote_copy(
            src_ref=pair_out.at[k], dst_ref=pair_in.at[k], send_sem=pair_sent.at[k],
            recv_sem=pair_got.at[k], device_id={"head": sibling}, device_id_type=MESH)

    def cross(k):
        return pltpu.make_async_remote_copy(
            src_ref=cross_out.at[k - 1], dst_ref=cross_in.at[k - 1], send_sem=cross_sent.at[k - 1],
            recv_sem=cross_got.at[k - 1], device_id={"section": peer(k)}, device_id_type=MESH)

    order = list(range(1, sections)) + [0]
    for k in range(1, sections):
        pair_out[k] = partial(peer(k), sibling)
        pair(k).start()
    for k in range(1, sections):
        mine = partial(peer(k), core)
        pair(k).wait_recv()
        cross_out[k - 1] = (mine + pair_in[k]).astype(BF16)
        cross(k).start()
    pair_out[0] = partial(section, sibling)
    pair(0).start()
    for h in range(heads):
        right = jnp.concatenate([up_[h], ds_in[h]], axis=0)
        grad = dot1(y_ref[h], right, TN)
        lanes = slice(h * width, (h + 1) * width)
        for b in range(tokens // HALF):
            t = slice(b * HALF, (b + 1) * HALF)
            g_ref[t, 0, lanes] = grad[b * BLK:b * BLK + HALF]
            g_ref[t, 1, lanes] = grad[b * BLK + HALF:(b + 1) * BLK]
    total = partial(section, core)
    pair(0).wait_recv()
    total = total + pair_in[0]
    for k in range(1, sections):
        cross(k).wait_recv()
        total = total + cross_in[k - 1].astype(F32)
    out_ref[...] = total.astype(BF16)
    for k in order:
        pair(k).wait_send()
    for k in range(1, sections):
        cross(k).wait_send()

    @pl.when(jnp.logical_not(last))
    def _():
        for h in range(heads):
            up(h).wait_send()

    @pl.when(jnp.logical_not(first))
    def _():
        for h in range(heads):
            down(h).wait_send()


def per_device(queries, reflect_keys, reflect_values, reflect_betas, decay_rates, resets,
               out_weight, out_cotangent):
    tokens = queries.shape[0]
    heads = reflect_betas.shape[2]
    width = queries.shape[1] // heads
    steps = 2 * tokens
    devices = lax.axis_size("seq")

    cot = lax.all_gather(out_cotangent, ("section", "head"), axis=1, tiled=True)

    group = 2 if heads % 2 == 0 else 1
    groups = heads // group
    marks = jnp.broadcast_to(resets.astype(F32)[None, None, :], (groups, 1, tokens))
    betas = reflect_betas.transpose(1, 2, 0).reshape(2, groups, group, tokens)
    rows = jnp.concatenate(
        [decay_rates.T.reshape(groups, group, tokens), marks, betas[0], betas[1],
         jnp.zeros((groups, 7 - 3 * group, tokens), F32)], axis=1)
    keys2 = reflect_keys.reshape(tokens, 2 * heads * width)
    values2 = reflect_values.reshape(tokens, 2 * heads * width)

    def whole(*shape):
        return pl.BlockSpec((1,) + shape, lambda h: (h,) + (0,) * len(shape))

    def several(*shape):
        return pl.BlockSpec((group,) + shape, lambda h: (h,) + (0,) * len(shape))

    def columns(offset):
        return pl.BlockSpec((tokens, group * width), lambda h: (0, h + offset))

    total = tokens + width
    y, r, m, o, b = pl.pallas_call(
        local_kernel,
        grid=(groups,),
        in_specs=[whole(8, tokens), columns(0), columns(0), columns(groups), columns(0), columns(groups)],
        out_specs=[several(total, steps), several(tokens, width), several(width, width),
                   several(tokens, width), several(width, width)],
        out_shape=[jax.ShapeDtypeStruct((heads, total, steps), BF16),
                   jax.ShapeDtypeStruct((heads, tokens, width), BF16),
                   jax.ShapeDtypeStruct((heads, width, width), F32),
                   jax.ShapeDtypeStruct((heads, tokens, width), F32),
                   jax.ShapeDtypeStruct((heads, width, width), F32)],
        compiler_params=pltpu.CompilerParams(vmem_limit_bytes=28 << 20),
        cost_estimate=pl.CostEstimate(flops=8 << 30, bytes_accessed=8 << 20, transcendentals=0),
        name="local",
    )(rows, queries, keys2, keys2, values2, values2)

    square = (heads, width, width)
    vmem = pl.BlockSpec(memory_space=pltpu.VMEM)
    dma = pltpu.SemaphoreType.DMA
    sections = lax.axis_size("section")
    features = out_weight.shape[1] // (2 * sections)
    output, value_grads = pl.pallas_call(
        functools.partial(tail_kernel, devices, sections),
        in_specs=[vmem] * 7,
        out_specs=[vmem] * 2,
        out_shape=[jax.ShapeDtypeStruct((features, tokens), BF16),
                   jax.ShapeDtypeStruct((tokens, 2, heads * width), F32)],
        scratch_shapes=[pltpu.VMEM(square, BF16)] * 4
        + [pltpu.VMEM(square, F32), pltpu.VMEM((heads, tokens, width), BF16)]
        + [pltpu.VMEM(square, BF16)] * 2
        + [pltpu.VMEM((heads * width, tokens), BF16),
           pltpu.VMEM((sections, features, tokens), F32),
           pltpu.VMEM((sections, features, tokens), F32),
           pltpu.VMEM((sections - 1, features, tokens), BF16),
           pltpu.VMEM((sections - 1, features, tokens), BF16)]
        + [dma((heads,))] * 4 + [dma((sections,))] * 2 + [dma((sections - 1,))] * 2,
        compiler_params=pltpu.CompilerParams(
            collective_id=0, has_side_effects=True, vmem_limit_bytes=24 << 20),
        name="tail",
    )(m, b, r, o, y, cot, out_weight)
    return output, value_grads


def solution(mesh):
    return jax.shard_map(
        per_device,
        mesh=mesh,
        in_specs=(
            P(("grp", "seq"), ("section", "head")),
            P(("grp", "seq"), None, ("section", "head")),
            P(("grp", "seq"), None, ("section", "head")),
            P(("grp", "seq"), None, ("section", "head")),
            P(("grp", "seq"), ("section", "head")),
            P(("grp", "seq")),
            P(("section", "head"), None),
            P(("grp", "seq"), ("section", "head")),
        ),
        out_specs=(
            P(("section", "head"), ("grp", "seq")),
            P(("grp", "seq"), None, ("section", "head")),
        ),
        check_vma=False,
    )
```

```python
import functools
import jax
import jax.numpy as jnp
from jax import lax
from jax.experimental import pallas as pl
from jax.experimental.pallas import tpu as pltpu
from jax.sharding import PartitionSpec as P

HALF = 64
BLK = 2 * HALF
F32 = jnp.float32
BF16 = jnp.bfloat16
NN = (((1,), (0,)), ((), ()))
NT = (((1,), (1,)), ((), ()))
TN = (((0,), (0,)), ((), ()))


def dot1(a, b, dims=NN):
    return lax.dot_general(a.astype(BF16), b.astype(BF16), dims, preferred_element_type=F32)


def halves(a):
    high = a.astype(BF16)
    return high, (a - high.astype(F32)).astype(BF16)


def dot3(a, b, dims=NN):
    ah, al = halves(a)
    bh, bl = halves(b)
    d = functools.partial(lax.dot_general, dimension_numbers=dims, preferred_element_type=F32)
    return d(ah, bh) + (d(ah, bl) + d(al, bh))


def iota(shape, axis):
    return lax.broadcasted_iota(jnp.int32, shape, axis)


def step_token(index):
    block, rest = index // BLK, index % BLK
    return block * HALF + rest % HALF, rest // HALF


def local_kernel(rows_ref, q_ref, k0_ref, k1_ref, v0_ref, v1_ref,
                 y_ref, r_ref, m_ref, o_ref, b_ref):
    group, width = m_ref.shape[0], m_ref.shape[1]
    tokens = q_ref.shape[0]
    blocks = tokens // HALF
    steps = 2 * tokens
    everything = [(g, b) for g in range(group) for b in range(blocks)]
    rows = rows_ref[0]
    top = rows.astype(BF16)
    rest = rows - top.astype(F32)
    middle = rest.astype(BF16)
    bottom = (rest - middle.astype(F32)).astype(BF16)
    tok_s, ref_s = step_token(iota((tokens, steps), 1))
    source = iota((tokens, steps), 0)
    upto = (source <= tok_s).astype(F32)
    before = (source <= tok_s + ref_s - 1).astype(F32)
    sums = dot1(jnp.concatenate([top.astype(F32), middle.astype(F32), bottom.astype(F32)], axis=0), before)
    c_rows = sums[0:8] + sums[8:16] + sums[16:24]
    z_rows = dot1(rows, upto)
    beta_rows = []
    for g in range(group):
        first, second = rows[1 + group + g:2 + group + g], rows[1 + 2 * group + g:2 + 2 * group + g]
        pieces = []
        for b in range(blocks):
            t = slice(b * HALF, (b + 1) * HALF)
            pieces += [first[:, t], second[:, t]]
        beta_rows.append(jnp.concatenate(pieces, axis=1))
    z_row = z_rows[group:group + 1]
    packed = jnp.concatenate(
        [c_rows[0:group], z_row] + beta_rows + [jnp.zeros((7 - 2 * group, steps), F32)], axis=0)
    packed_cols = packed.T
    z_col = packed_cols[:, group:group + 1]
    c_row = [c_rows[g:g + 1] for g in range(group)]
    c_col = [packed_cols[:, g:g + 1] for g in range(group)]
    beta_col = [packed_cols[:, group + 1 + g:group + 2 + g] for g in range(group)]
    z_end = z_row[:, steps - 1:]

    def sl(b):
        return slice(b * BLK, (b + 1) * BLK)

    def lanes(g):
        return slice(g * width, (g + 1) * width)

    keys, values = {}, {}
    for g, b in everything:
        t = slice(b * HALF, (b + 1) * HALF)
        keys[g, b] = jnp.concatenate([k0_ref[t, lanes(g)], k1_ref[t, lanes(g)]], axis=0)
        values[g, b] = jnp.concatenate([v0_ref[t, lanes(g)], v1_ref[t, lanes(g)]], axis=0)
    eye = iota((BLK, BLK), 0) == iota((BLK, BLK), 1)
    identity = jnp.where(eye, 1.0, 0.0)
    tm_r = 2 * (iota((BLK, BLK), 0) % HALF) + iota((BLK, BLK), 0) // HALF
    tm_c = 2 * (iota((BLK, BLK), 1) % HALF) + iota((BLK, BLK), 1) // HALF

    low, scale_row, scale_col, gram = {}, {}, {}, {}
    for g, b in everything:
        for c in range(b + 1):
            gram[g, b, c] = dot1(keys[g, b], keys[g, c], NT)
    for g, b in everything:
        diag = jnp.where(eye, gram[g, b, b], 0.0)
        scale_row[g, b] = lax.rsqrt(jnp.sum(diag, axis=0, keepdims=True) + 1e-6)
        scale_col[g, b] = lax.rsqrt(jnp.sum(diag, axis=1, keepdims=True) + 1e-6)
    for g, b in everything:
        left = beta_col[g][sl(b)] * scale_col[g, b]
        for c in range(b + 1):
            valid = z_col[sl(b)] == z_row[:, sl(c)]
            if b == c:
                valid = valid & (tm_r > tm_c)
            gap = jnp.where(valid, c_row[g][:, sl(c)] - c_col[g][sl(b)], 0.0)
            low[g, b, c] = jnp.where(
                valid, jnp.exp(gap) * gram[g, b, c] * left * scale_row[g, c], 0.0)

    rounded = {i: low[i[0], i[1], i[1]].astype(BF16) for i in everything}
    inverse = {i: identity - jnp.where((tm_r >> 1) == (tm_c >> 1), low[i[0], i[1], i[1]], 0.0)
               for i in everything}
    level = 2
    while (1 << level) <= BLK:
        pick = ((tm_r >> level) == (tm_c >> level)) & ((tm_r >> (level - 1)) != (tm_c >> (level - 1)))
        narrow = {i: inverse[i].astype(BF16) for i in everything}
        inner = {i: dot1(jnp.where(pick, rounded[i], jnp.zeros_like(rounded[i])), narrow[i])
                 for i in everything}
        inverse = {i: inverse[i] - dot1(narrow[i], inner[i]) for i in everything}
        level += 1
    for _ in range(2):
        residual = {i: dot3(low[i[0], i[1], i[1]], inverse[i]) + (inverse[i] - identity)
                    for i in everything}
        inverse = {i: inverse[i] - dot1(inverse[i], residual[i]) for i in everything}

    gamma_end_row = [jnp.where(z_row == z_end, jnp.exp(c_row[g] - c_row[g][:, steps - 1:]), 0.0)
                     for g in range(group)]
    solved = {}
    for b in reversed(range(blocks)):
        for g in range(group):
            parts = []
            for a in range(b, blocks):
                t = slice(a * HALF, (a + 1) * HALF)
                product = dot1(q_ref[t, lanes(g)], keys[g, b], NT)
                second = slice(a * BLK + HALF, (a + 1) * BLK)
                valid = z_col[second] == z_row[:, sl(b)]
                if a == b:
                    valid = valid & (iota((HALF, BLK), 0) >= iota((HALF, BLK), 1) % HALF)
                gap = jnp.where(valid, c_row[g][:, sl(b)] - c_col[g][second], 0.0)
                parts.append(jnp.where(valid, jnp.exp(gap) * product * scale_row[g, b], 0.0))
            parts.append(keys[g, b].astype(F32).T * (scale_row[g, b] * gamma_end_row[g][:, sl(b)]))
            x = jnp.concatenate(parts, axis=0)
            if b + 1 < blocks:
                later = []
                for c in range(b + 1, blocks):
                    later.append(jnp.concatenate(
                        [jnp.zeros(((c - b) * HALF, BLK), F32), solved[g, c]], axis=0))
                x = x - dot3(jnp.concatenate(later, axis=1),
                             jnp.concatenate([low[g, c, b] for c in range(b + 1, blocks)], axis=0))
            solved[g, b] = dot3(x, inverse[g, b])

    total = tokens + width
    for g in range(group):
        gamma_row = jnp.where(z_row == 0, jnp.exp(-c_row[g]), 0.0)
        plain, moved, gamma_tok = [], [], []
        for b in range(blocks):
            y = solved[g, b] * packed[group + 1 + g:group + 2 + g, sl(b)]
            if b:
                y = jnp.concatenate([jnp.zeros((b * HALF, BLK), F32), y], axis=0)
            y_ref[g, :, sl(b)] = y.astype(BF16)
            plain.append(y.astype(BF16))
            moved.append((y * (gamma_row[:, sl(b)] * scale_row[g, b])).astype(BF16))
            second = slice(b * BLK + HALF, (b + 1) * BLK)
            gamma_tok.append(jnp.where(z_col[second] == 0, jnp.exp(-c_col[g][second]), 0.0))
        plain = dot1(jnp.concatenate(plain, axis=1),
                     jnp.concatenate([values[g, b] for b in range(blocks)], axis=0))
        moved = dot1(jnp.concatenate(moved, axis=1),
                     jnp.concatenate([keys[g, b] for b in range(blocks)], axis=0))
        o_ref[g] = plain[:tokens]
        b_ref[g] = plain[tokens:]
        gamma_tok = jnp.concatenate(gamma_tok, axis=0)
        r_ref[g] = (gamma_tok * q_ref[:, lanes(g)].astype(F32) - moved[:tokens]).astype(BF16)
        gamma_end = jnp.where(z_end == 0, jnp.exp(-c_row[g][:, steps - 1:]), 0.0)
        m_ref[g] = jnp.where(iota((width, width), 0) == iota((width, width), 1), gamma_end, 0.0) - moved[tokens:]


MESH = pl.DeviceIdType.MESH


def tail_kernel(devices, sections, m_hbm, b_hbm, r_hbm, o_hbm, y_hbm, cot_hbm, w_hbm,
                out_ref, g_ref,
                m_ref, b_ref, r_ref, o_ref, y_ref, cot_ref, w_ref, loaded,
                s_in, s_out, ds_in, ds_out, d, up_, mh, ml,
                mixed, pair_out, pair_in, cross_out, cross_in,
                s_sent, s_got, ds_sent, ds_got, pair_sent, pair_got, cross_sent, cross_got):
    heads, tokens, width = r_ref.shape
    features = out_ref.shape[0]
    pairs = ((m_hbm, m_ref), (b_hbm, b_ref), (cot_hbm, cot_ref), (w_hbm, w_ref), (r_hbm, r_ref),
             (o_hbm, o_ref), (y_hbm, y_ref))
    loads = [pltpu.make_async_copy(a, c, loaded.at[i]) for i, (a, c) in enumerate(pairs)]
    for load in loads:
        load.start()
    place = lax.axis_index("seq")
    section, core = lax.axis_index("section"), lax.axis_index("head")
    sibling = 1 - core
    first, last = place == 0, place == devices - 1

    def peer(k):
        return lax.rem(section + k, sections)

    barrier = pltpu.get_barrier_semaphore()

    @pl.when(jnp.logical_not(first))
    def _():
        pl.semaphore_signal(barrier, inc=1, device_id={"seq": place - 1}, device_id_type=MESH)

    @pl.when(jnp.logical_not(last))
    def _():
        pl.semaphore_signal(barrier, inc=1, device_id={"seq": place + 1}, device_id_type=MESH)

    pl.semaphore_signal(barrier, inc=1, device_id={"head": sibling}, device_id_type=MESH)
    for k in range(1, sections):
        pl.semaphore_signal(barrier, inc=1, device_id={"section": peer(k)}, device_id_type=MESH)
    loads[0].wait()
    loads[1].wait()
    for h in range(heads):
        mh[h], ml[h] = halves(m_ref[h])
    pl.semaphore_wait(barrier, sections + jnp.where(first, 0, 1) + jnp.where(last, 0, 1))

    def up(h):
        return pltpu.make_async_remote_copy(
            src_ref=s_out.at[h], dst_ref=s_in.at[h], send_sem=s_sent.at[h], recv_sem=s_got.at[h],
            device_id={"seq": place + 1}, device_id_type=MESH)

    def down(h):
        return pltpu.make_async_remote_copy(
            src_ref=ds_out.at[h], dst_ref=ds_in.at[h], send_sem=ds_sent.at[h], recv_sem=ds_got.at[h],
            device_id={"seq": place - 1}, device_id_type=MESH)

    def forward():
        for h in range(heads):
            @pl.when(first)
            def _():
                s_in[h] = jnp.zeros(s_in.shape[1:], BF16)

            @pl.when(jnp.logical_not(first))
            def _():
                up(h).wait_recv()

            @pl.when(jnp.logical_not(last))
            def _():
                s = s_in[h]
                s_out[h] = (dot1(mh[h], s) + dot1(ml[h], s) + b_ref[h]).astype(BF16)
                up(h).start()

    def backward():
        for h in range(heads):
            @pl.when(last)
            def _():
                ds_in[h] = jnp.zeros(ds_in.shape[1:], BF16)

            @pl.when(jnp.logical_not(last))
            def _():
                down(h).wait_recv()

            @pl.when(jnp.logical_not(first))
            def _():
                ds = ds_in[h]
                ds_out[h] = (dot1(mh[h], ds, TN) + dot1(ml[h], ds, TN) + d[h]).astype(BF16)
                down(h).start()

    low = 2 * place < devices

    @pl.when(low)
    def _():
        forward()

    for i in (2, 3, 4):
        loads[i].wait()
    for h in range(heads):
        upstream = dot1(cot_ref[...], w_ref[h * width:(h + 1) * width, :], NT).astype(BF16)
        up_[h] = upstream
        d[h] = dot1(r_ref[h], upstream, TN)

    @pl.when(low)
    def _():
        backward()

    @pl.when(jnp.logical_not(low))
    def _():
        backward()
        forward()

    loads[5].wait()
    for h in range(heads):
        mixed[h * width:(h + 1) * width, :] = (dot1(r_ref[h], s_in[h]) + o_ref[h]).T.astype(BF16)

    def partial(target, side):
        start = pl.multiple_of((target * 2 + side) * features, 128)
        return dot1(w_ref[:, pl.ds(start, features)], mixed[...], TN)

    def pair(k):
        return pltpu.make_async_remote_copy(
            src_ref=pair_out.at[k], dst_ref=pair_in.at[k], send_sem=pair_sent.at[k],
            recv_sem=pair_got.at[k], device_id={"head": sibling}, device_id_type=MESH)

    def cross(k):
        return pltpu.make_async_remote_copy(
            src_ref=cross_out.at[k - 1], dst_ref=cross_in.at[k - 1], send_sem=cross_sent.at[k - 1],
            recv_sem=cross_got.at[k - 1], device_id={"section": peer(k)}, device_id_type=MESH)

    order = list(range(1, sections)) + [0]
    for k in range(1, sections):
        pair_out[k] = partial(peer(k), sibling)
        pair(k).start()
    for k in range(1, sections):
        mine = partial(peer(k), core)
        pair(k).wait_recv()
        cross_out[k - 1] = (mine + pair_in[k]).astype(BF16)
        cross(k).start()
    pair_out[0] = partial(section, sibling)
    pair(0).start()
    loads[6].wait()
    for h in range(heads):
        right = jnp.concatenate([up_[h], ds_in[h]], axis=0)
        grad = dot1(y_ref[h], right, TN)
        lanes = slice(h * width, (h + 1) * width)
        for b in range(tokens // HALF):
            t = slice(b * HALF, (b + 1) * HALF)
            g_ref[t, 0, lanes] = grad[b * BLK:b * BLK + HALF]
            g_ref[t, 1, lanes] = grad[b * BLK + HALF:(b + 1) * BLK]
    total = partial(section, core)
    pair(0).wait_recv()
    total = total + pair_in[0]
    for k in range(1, sections):
        cross(k).wait_recv()
        total = total + cross_in[k - 1].astype(F32)
    out_ref[...] = total.astype(BF16)
    for k in order:
        pair(k).wait_send()
    for k in range(1, sections):
        cross(k).wait_send()

    @pl.when(jnp.logical_not(last))
    def _():
        for h in range(heads):
            up(h).wait_send()

    @pl.when(jnp.logical_not(first))
    def _():
        for h in range(heads):
            down(h).wait_send()


def per_device(queries, reflect_keys, reflect_values, reflect_betas, decay_rates, resets,
               out_weight, out_cotangent):
    tokens = queries.shape[0]
    heads = reflect_betas.shape[2]
    width = queries.shape[1] // heads
    steps = 2 * tokens
    devices = lax.axis_size("seq")

    cot = lax.all_gather(out_cotangent, ("section", "head"), axis=1, tiled=True)

    group = 2 if heads % 2 == 0 else 1
    groups = heads // group
    marks = jnp.broadcast_to(resets.astype(F32)[None, None, :], (groups, 1, tokens))
    betas = reflect_betas.transpose(1, 2, 0).reshape(2, groups, group, tokens)
    rows = jnp.concatenate(
        [decay_rates.T.reshape(groups, group, tokens), marks, betas[0], betas[1],
         jnp.zeros((groups, 7 - 3 * group, tokens), F32)], axis=1)
    keys2 = reflect_keys.reshape(tokens, 2 * heads * width)
    values2 = reflect_values.reshape(tokens, 2 * heads * width)

    def whole(*shape):
        return pl.BlockSpec((1,) + shape, lambda h: (h,) + (0,) * len(shape))

    def several(*shape):
        return pl.BlockSpec((group,) + shape, lambda h: (h,) + (0,) * len(shape))

    def columns(offset):
        return pl.BlockSpec((tokens, group * width), lambda h: (0, h + offset))

    total = tokens + width
    y, r, m, o, b = pl.pallas_call(
        local_kernel,
        grid=(groups,),
        in_specs=[whole(8, tokens), columns(0), columns(0), columns(groups), columns(0), columns(groups)],
        out_specs=[several(total, steps), several(tokens, width), several(width, width),
                   several(tokens, width), several(width, width)],
        out_shape=[jax.ShapeDtypeStruct((heads, total, steps), BF16),
                   jax.ShapeDtypeStruct((heads, tokens, width), BF16),
                   jax.ShapeDtypeStruct((heads, width, width), F32),
                   jax.ShapeDtypeStruct((heads, tokens, width), F32),
                   jax.ShapeDtypeStruct((heads, width, width), F32)],
        compiler_params=pltpu.CompilerParams(vmem_limit_bytes=58 << 20),
        cost_estimate=pl.CostEstimate(flops=8 << 30, bytes_accessed=8 << 20, transcendentals=0),
        name="local",
    )(rows, queries, keys2, keys2, values2, values2)

    square = (heads, width, width)
    vmem = pl.BlockSpec(memory_space=pltpu.VMEM)
    dma = pltpu.SemaphoreType.DMA
    sections = lax.axis_size("section")
    features = out_weight.shape[1] // (2 * sections)
    output, value_grads = pl.pallas_call(
        functools.partial(tail_kernel, devices, sections),
        in_specs=[pl.BlockSpec(memory_space=pl.ANY)] * 7,
        out_specs=[vmem] * 2,
        out_shape=[jax.ShapeDtypeStruct((features, tokens), BF16),
                   jax.ShapeDtypeStruct((tokens, 2, heads * width), F32)],
        scratch_shapes=[pltpu.VMEM(a.shape, a.dtype) for a in (m, b, r, o, y, cot, out_weight)]
        + [dma((7,))] + [pltpu.VMEM(square, BF16)] * 4
        + [pltpu.VMEM(square, F32), pltpu.VMEM((heads, tokens, width), BF16)]
        + [pltpu.VMEM(square, BF16)] * 2
        + [pltpu.VMEM((heads * width, tokens), BF16),
           pltpu.VMEM((sections, features, tokens), F32),
           pltpu.VMEM((sections, features, tokens), F32),
           pltpu.VMEM((sections - 1, features, tokens), BF16),
           pltpu.VMEM((sections - 1, features, tokens), BF16)]
        + [dma((heads,))] * 4 + [dma((sections,))] * 2 + [dma((sections - 1,))] * 2,
        compiler_params=pltpu.CompilerParams(
            collective_id=0, has_side_effects=True, vmem_limit_bytes=58 << 20),
        name="tail",
    )(m, b, r, o, y, cot, out_weight)
    return output, value_grads


def solution(mesh):
    return jax.shard_map(
        per_device,
        mesh=mesh,
        in_specs=(
            P(("grp", "seq"), ("section", "head")),
            P(("grp", "seq"), None, ("section", "head")),
            P(("grp", "seq"), None, ("section", "head")),
            P(("grp", "seq"), None, ("section", "head")),
            P(("grp", "seq"), ("section", "head")),
            P(("grp", "seq")),
            P(("section", "head"), None),
            P(("grp", "seq"), ("section", "head")),
        ),
        out_specs=(
            P(("section", "head"), ("grp", "seq")),
            P(("grp", "seq"), None, ("section", "head")),
        ),
        check_vma=False,
    )
```
